512 devices in a mesh: gx: 32 (over x, z), gy: 8 (over y_lo, core), phys: 2 (over y_hi).
Axes of the slice: x: 4, y: 8 (y_hi: 2, y_lo: 4; y = y_hi * 4 + y_lo), z: 8, core: 2. Of those that a mesh axis runs over, the one named last changes fastest.
Arguments:
- mech_load: float32 [32, 8, 2, 128, 768], P('gx', 'gy', 'phys'), may hold values from -63 to 63
- heat_load: float32 [32, 8, 2, 128, 256], P('gx', 'gy', 'phys'), may hold values from -63 to 63
- mech_factor: bfloat16 [32, 8, 2, 768, 768], P('gx', 'gy', 'phys'), may hold values from -0.21875 to 0.21875
- heat_factor: bfloat16 [32, 8, 2, 256, 256], P('gx', 'gy', 'phys'), may hold values from -0.375 to 0.375
- mech_diag: float32 [32, 8, 2, 768], P('gx', 'gy', 'phys'), may hold values from 0.1 to 1
- heat_diag: float32 [32, 8, 2, 256], P('gx', 'gy', 'phys'), may hold values from 0.1 to 1
- mech_wx: float32 [32, 8, 2, 768], P('gx', 'gy', 'phys'), may hold values from 0.5 to 4
- mech_wy: float32 [32, 8, 2, 768], P('gx', 'gy', 'phys'), may hold values from 0.5 to 4
- mech_wp: float32 [32, 8, 768], P('gx', 'gy'), may hold values from 0.5 to 4
- heat_wx: float32 [32, 8, 2, 256], P('gx', 'gy', 'phys'), may hold values from 0.5 to 4
- heat_wy: float32 [32, 8, 2, 256], P('gx', 'gy', 'phys'), may hold values from 0.5 to 4
- heat_wp: float32 [32, 8, 256], P('gx', 'gy'), may hold values from 0.5 to 4
- coupling: bfloat16 [32, 8, 2, 768, 256], P('gx', 'gy', 'phys'), may hold values from -0.21875 to 0.21875
- mech_sens: bfloat16 [32, 8, 2, 768, 256], P('gx', 'gy', 'phys'), may hold values from -0.21875 to 0.21875
- heat_sens: bfloat16 [32, 8, 2, 256, 256], P('gx', 'gy', 'phys'), may hold values from -0.375 to 0.375
- density: float32 [32, 8, 256], P('gx', 'gy', 'phys'), may hold values from 0.2 to 1
- material_ids: int32 [32, 8, 256], P('gx', 'gy', 'phys'), may hold values from 0 to 7
- material_scale: float32 [8], replicated, may hold values from 1 to 10
Outputs:
- mech_adjoint: float32 [32, 8, 2, 128, 768], P('gx', 'gy', 'phys')
- heat_adjoint: float32 [32, 8, 2, 128, 256], P('gx', 'gy', 'phys')
- gradient: float32 [32, 8, 256], P('gx', 'gy', 'phys')
The draws below stay inside these ranges and needn't reach their ends.
All inputs are finite; a program needn't handle non-finite values.
Results may differ from the reference program's by a relative error of at most 0.014.
Values may be sent and summed in bfloat16 or wider, within the bound.
A program may use at most 64 MiB of HBM per device.

```python
import math
import jax
import jax.numpy as jnp
from jax import lax

FN = 256
RM = 768
LOADS = 128
NDES = 256
NMAT = 8
ITERS = 2
FACES = 2
NSX = 32
NSY = 8


def ramp_load(key, width):
    dimensions = (NSX, NSY, FACES, LOADS, width)
    first, second = jax.random.split(key)
    along_x = jnp.arange(NSX, dtype=jnp.float32) / max(NSX - 1, 1)
    along_y = jnp.arange(NSY, dtype=jnp.float32) / max(NSY - 1, 1)
    growth = (1.0 + 2.0 * along_x)[:, None] * (1.0 + 2.0 * along_y)[None, :]
    values = jnp.clip(jax.random.normal(first, dimensions, jnp.float32), -4.0, 4.0)
    column = jnp.exp(jax.random.uniform(second, (LOADS,), jnp.float32, 0.0, math.log(4.0)))
    return 0.3 * values * column[None, None, None, :, None] * growth[:, :, None, None, None]


def draw_mech_load(key, part):
    return ramp_load(jax.random.fold_in(key, 11), RM)


def draw_heat_load(key, part):
    return ramp_load(jax.random.fold_in(key, 12), FN)


def touch_ends(entries, own_key, low, largest):
    longest = entries.shape.index(max(entries.shape))
    spots = []
    for shift in (0, 1):
        where = [jax.random.randint(jax.random.fold_in(own_key, axis), (), 0, length) for axis, length in enumerate(entries.shape)]
        where[longest] = (where[longest] + shift) % entries.shape[longest]
        spots.append(tuple(where))
    return entries.at[spots[0]].set(low).at[spots[1]].set(largest)


def level_of(own_key, extent, cuts, least, top_value):
    gain = 1.0
    for dim, parts in cuts:
        steps = jax.random.uniform(jax.random.fold_in(jax.random.fold_in(own_key, 6), dim), (parts,), jnp.float32, least / len(cuts), top_value / len(cuts))
        gain = gain * jnp.repeat(jnp.exp(steps), extent[dim] // parts).reshape((-1,) + (1,) * (len(extent) - 1 - dim))
    return gain


def bell_draw(own_key, dims, scale, bound, cuts=(), held_as=jnp.bfloat16):
    values = scale * jax.random.normal(own_key, dims, jnp.float32)
    if cuts:
        values = values * level_of(own_key, dims, cuts, -0.22, 0.18)
    return jnp.clip(values, -bound, bound).astype(held_as)


def setup_inputs(seed: int = 0) -> dict:
    key_of = jax.random.split(jax.random.key(seed), 19)
    mech_load = draw_mech_load(jax.random.fold_in(key_of[18], 71), 0)
    heat_load = draw_heat_load(jax.random.fold_in(key_of[18], 71), 0)
    mech_factor = bell_draw(key_of[2], (NSX, NSY, FACES, RM, RM), RM ** -0.5, 0.21875, ((0, 32), (1, 8), (2, 2)))
    heat_factor = bell_draw(key_of[3], (NSX, NSY, FACES, FN, FN), FN ** -0.5, 0.375, ((0, 32), (1, 8), (2, 2)))
    mech_diag = jnp.clip(jnp.exp(math.log(1.0) - 2.3025851 * jax.random.uniform(key_of[4], (NSX, NSY, FACES, RM), jnp.float32) ** level_of(key_of[4], (NSX, NSY, FACES, RM), ((0, 32), (1, 8), (2, 2)), -0.2, 0.2)), 0.1, 1.0)
    heat_diag = jnp.clip(jnp.exp(math.log(1.0) - 2.3025851 * jax.random.uniform(key_of[5], (NSX, NSY, FACES, FN), jnp.float32) ** level_of(key_of[5], (NSX, NSY, FACES, FN), ((0, 32), (1, 8), (2, 2)), -0.2, 0.2)), 0.1, 1.0)
    mech_wx = jnp.clip(jnp.exp(math.log(4.0) - 2.0794415 * jax.random.uniform(key_of[6], (NSX, NSY, FACES, RM), jnp.float32) ** level_of(key_of[6], (NSX, NSY, FACES, RM), ((0, 32), (1, 8), (2, 2)), -0.2, 0.2)), 0.5, 4.0)
    mech_wy = jnp.clip(jnp.exp(math.log(4.0) - 2.0794415 * jax.random.uniform(key_of[7], (NSX, NSY, FACES, RM), jnp.float32) ** level_of(key_of[7], (NSX, NSY, FACES, RM), ((0, 32), (1, 8), (2, 2)), -0.2, 0.2)), 0.5, 4.0)
    mech_wp = jnp.clip(jnp.exp(math.log(4.0) - 2.0794415 * jax.random.uniform(key_of[8], (NSX, NSY, RM), jnp.float32) ** level_of(key_of[8], (NSX, NSY, RM), ((0, 32), (1, 8)), -0.2, 0.2)), 0.5, 4.0)
    heat_wx = jnp.clip(jnp.exp(math.log(4.0) - 2.0794415 * jax.random.uniform(key_of[9], (NSX, NSY, FACES, FN), jnp.float32) ** level_of(key_of[9], (NSX, NSY, FACES, FN), ((0, 32), (1, 8), (2, 2)), -0.2, 0.2)), 0.5, 4.0)
    heat_wy = jnp.clip(jnp.exp(math.log(4.0) - 2.0794415 * jax.random.uniform(key_of[10], (NSX, NSY, FACES, FN), jnp.float32) ** level_of(key_of[10], (NSX, NSY, FACES, FN), ((0, 32), (1, 8), (2, 2)), -0.2, 0.2)), 0.5, 4.0)
    heat_wp = jnp.clip(jnp.exp(math.log(4.0) - 2.0794415 * jax.random.uniform(key_of[11], (NSX, NSY, FN), jnp.float32) ** level_of(key_of[11], (NSX, NSY, FN), ((0, 32), (1, 8)), -0.2, 0.2)), 0.5, 4.0)
    coupling = bell_draw(key_of[12], (NSX, NSY, FACES, RM, FN), RM ** -0.5, 0.21875, ((0, 32), (1, 8), (2, 2)))
    mech_sens = bell_draw(key_of[13], (NSX, NSY, FACES, RM, NDES), RM ** -0.5, 0.21875, ((0, 32), (1, 8), (2, 2)))
    heat_sens = bell_draw(key_of[14], (NSX, NSY, FACES, FN, NDES), FN ** -0.5, 0.375, ((0, 32), (1, 8), (2, 2)))
    density = jnp.clip(0.2 + 0.8 * jax.random.uniform(key_of[15], (NSX, NSY, NDES), jnp.float32) ** level_of(key_of[15], (NSX, NSY, NDES), ((0, 32), (1, 8), (2, 2)), -0.2, 0.2), 0.2, 1.0)
    material_ids = touch_ends(jax.random.randint(key_of[16], (NSX, NSY, NDES), 0, NMAT), jax.random.fold_in(key_of[16], 1), 0, NMAT - 1).astype(jnp.int32)
    material_scale = jnp.clip(jnp.exp(jax.random.uniform(key_of[17], (NMAT,), jnp.float32, math.log(1.0), math.log(10.0))), 1.0, 10.0)
    return dict(mech_load=mech_load, heat_load=heat_load, mech_factor=mech_factor, heat_factor=heat_factor, mech_diag=mech_diag, heat_diag=heat_diag, mech_wx=mech_wx, mech_wy=mech_wy, mech_wp=mech_wp, heat_wx=heat_wx, heat_wy=heat_wy, heat_wp=heat_wp, coupling=coupling, mech_sens=mech_sens, heat_sens=heat_sens, density=density, material_ids=material_ids, material_scale=material_scale)


def from_lower(values, dimension):
    filler = jnp.zeros_like(lax.slice_in_dim(values, 0, 1, axis=dimension))
    kept = lax.slice_in_dim(values, 0, values.shape[dimension] - 1, axis=dimension)
    return jnp.concatenate([filler, kept], axis=dimension)


def from_upper(values, dimension):
    filler = jnp.zeros_like(lax.slice_in_dim(values, 0, 1, axis=dimension))
    kept = lax.slice_in_dim(values, 1, values.shape[dimension], axis=dimension)
    return jnp.concatenate([kept, filler], axis=dimension)


def apply_operator(rounded, factor, diagonal, edge_x, edge_y, edge_phys):
    flat_dirs = rounded.reshape((-1,) + rounded.shape[3:])
    flat_factors = factor.reshape((-1,) + factor.shape[3:])

    def block_schur(inputs):
        block_dir, block_factor = inputs
        inner = jnp.dot(block_dir, block_factor, preferred_element_type=jnp.float32).astype(jnp.bfloat16)
        return jnp.dot(inner, block_factor.T, preferred_element_type=jnp.float32)

    schur = lax.map(block_schur, (flat_dirs, flat_factors)).reshape(rounded.shape)
    values = rounded.astype(jnp.float32)
    lower_x = edge_x[:, :, :, None, :]
    upper_x = from_upper(lower_x, 0)
    lower_y = edge_y[:, :, :, None, :]
    upper_y = from_upper(lower_y, 1)
    image = schur + diagonal[:, :, :, None, :] * values
    image = image + lower_x * (values - from_lower(values, 0)) + upper_x * (values - from_upper(values, 0))
    image = image + lower_y * (values - from_lower(values, 1)) + upper_y * (values - from_upper(values, 1))
    image = image + edge_phys[:, :, None, None, :] * (values - values[:, :, ::-1])
    return image


def interface_solve(load, factor, diagonal, edge_x, edge_y, edge_phys):
    summed_axes = (0, 1, 2, 4)
    solution = jnp.zeros_like(load)
    residual = load
    direction = load
    current = jnp.sum(residual * residual, axis=summed_axes)
    for iteration in range(ITERS):
        rounded = direction.astype(jnp.bfloat16)
        image = apply_operator(rounded, factor, diagonal, edge_x, edge_y, edge_phys)
        curvature = jnp.sum(rounded.astype(jnp.float32) * image, axis=summed_axes)
        alpha = (current / curvature)[None, None, None, :, None]
        solution = solution + alpha * direction
        if iteration + 1 < ITERS:
            residual = residual - alpha * image
            following = jnp.sum(residual * residual, axis=summed_axes)
            direction = residual + (following / current)[None, None, None, :, None] * direction
            current = following
    return solution


def reference(mech_load, heat_load, mech_factor, heat_factor, mech_diag, heat_diag, mech_wx, mech_wy, mech_wp, heat_wx, heat_wy, heat_wp, coupling, mech_sens, heat_sens, density, material_ids, material_scale):
    mech_adjoint = interface_solve(mech_load, mech_factor, mech_diag, mech_wx, mech_wy, mech_wp)
    flat_adjoint = mech_adjoint.astype(jnp.bfloat16).reshape((-1,) + mech_adjoint.shape[3:])
    flat_coupling = coupling.reshape((-1,) + coupling.shape[3:])

    def block_couple(inputs):
        block_adj, block_coupling = inputs
        return jnp.dot(block_adj, block_coupling, preferred_element_type=jnp.float32)

    coupled = lax.map(block_couple, (flat_adjoint, flat_coupling)).reshape(heat_load.shape)
    heat_source = heat_load - coupled
    heat_adjoint = interface_solve(heat_source, heat_factor, heat_diag, heat_wx, heat_wy, heat_wp)
    mech_energy = jnp.sum(mech_adjoint * mech_adjoint, axis=3).astype(jnp.bfloat16)
    heat_energy = jnp.sum(heat_adjoint * heat_adjoint, axis=3).astype(jnp.bfloat16)
    sensitivity = jnp.einsum("abpr,abprd->abd", mech_energy.astype(jnp.float32), mech_sens.astype(jnp.float32), precision=lax.Precision.HIGHEST)
    sensitivity = sensitivity + jnp.einsum("abpr,abprd->abd", heat_energy.astype(jnp.float32), heat_sens.astype(jnp.float32), precision=lax.Precision.HIGHEST)
    stiffness = material_scale[material_ids]
    gradient = -3.0 * density * density * stiffness * sensitivity / LOADS
    return mech_adjoint, heat_adjoint, gradient
```

```python
import functools

import jax
import jax.numpy as jnp
from jax import lax
from jax.experimental import pallas as pl
from jax.experimental.pallas import tpu as pltpu
from jax.sharding import PartitionSpec as P

MESH = pl.DeviceIdType.MESH
F32 = jnp.float32
BF16 = jnp.bfloat16
ROWS = 16
LOADS = 128
HALF = LOADS // 2


def ring(k, n):
    return min(k, n - k)


def remote(src, dst, send, recv, peer):
    return pltpu.make_async_remote_copy(
        src_ref=src, dst_ref=dst, send_sem=send, recv_sem=recv, device_id=peer, device_id_type=MESH
    )


def row_loop(body):
    def step(n, carry):
        body(pl.ds(pl.multiple_of(n * ROWS, ROWS), ROWS))
        return carry

    lax.fori_loop(0, LOADS // ROWS, step, 0)


def lanes(x):
    return jnp.sum(x, axis=1, keepdims=True)


def times(a, b):
    return jnp.dot(a, b, preferred_element_type=F32)


def times_t(a, b):
    return lax.dot_general(a, b, (((1,), (1,)), ((), ())), preferred_element_type=F32)


def step_sizes(total):
    rr, rw, ww, gw, hw = (total[k : k + 1, :] for k in range(5))
    alpha = rr / rw
    beta = (rr - 2.0 * alpha * rw + alpha * alpha * ww) / rr
    grow = 1.0 + beta
    curve = grow * grow * rw - 2.0 * grow * alpha * gw + alpha * alpha * hw
    second = beta * rr / curve
    return alpha + second * grow, -second * alpha


def kernel(
    nx, ny, xs, zs,
    ml, hl, mf, hf, md, hd, mx, my, mp, hx, hy, hp, cp, ms, hs, dn, ids, scale,
    out_m, out_h, out_g,
    r0, h0, zf, bf, mw, hw, mup, hup, cf, sm, sh, den, mat,
    q0, qn, w0, wb, wn, hu, hun, uf, bhu, vf, vb, vn, bv, s0, bs, bsb, bsn,
    msc, col, mom, arx1, ary1, arx2, ary2, xm, xh, sp, sr,
    lsem, osem, wsend, wrecv, esend, erecv, asend, arecv, fsem,
):
    i, j, f = lax.axis_index("gx"), lax.axis_index("gy"), lax.axis_index("phys")
    low_x, high_x, low_y, high_y = i > 0, i < nx - 1, j > 0, j < ny - 1
    up_x = (jnp.minimum(i + 1, nx - 1), j, f)
    down_x = (jnp.maximum(i - 1, 0), j, f)
    up_y = (i, jnp.minimum(j + 1, ny - 1), f)
    down_y = (i, jnp.maximum(j - 1, 0), f)
    other = (i, j, 1 - f)
    target = (up_x, down_x, up_y, down_y, other)
    sends = (high_x, low_x, high_y, low_y, None)
    gets = (low_x, high_x, low_y, high_y, None)

    def guarded(cond, fn):
        if cond is None:
            fn()
        else:
            pl.when(cond)(fn)

    xi, zi = lax.div(i, zs), lax.rem(i, zs)
    offsets = [(a, b) for a in range(xs) for b in range(zs) if (a, b) != (0, 0)]
    offsets.sort(key=lambda o: -(ring(o[0], xs) + ring(o[1], zs)))
    x_peers = [(lax.rem(xi + a, xs) * zs + lax.rem(zi + b, zs), j, f) for a, b in offsets]
    n_yp = ny * 2
    yi, ci = f * (ny // 2) + lax.div(j, 2), lax.rem(j, 2)
    offsets = [(a, b) for a in range(ny) for b in range(2) if (a, b) != (0, 0)]
    offsets.sort(key=lambda o: -(ring(o[0], ny) + 0.1 * o[1]))
    y_peers = []
    for a, b in offsets:
        y = lax.rem(yi + a, ny)
        y_peers.append((i, lax.rem(y, ny // 2) * 2 + lax.rem(ci + b, 2), lax.div(y, ny // 2)))
    x_slot, y_slot = i, yi * 2 + ci

    loads = []

    def load(src, dst):
        copy = pltpu.make_async_copy(src, dst, lsem.at[len(loads)])
        copy.start()
        loads.append(copy)
        return copy

    get_r0 = load(ml.at[0, 0, 0], r0)
    small = [
        load(md.at[0, 0], mw.at[0]), load(mx.at[0, 0], mw.at[1]), load(my.at[0, 0], mw.at[2]),
        load(mp.at[0], mw.at[3]),
        load(hd.at[0, 0], hw.at[0]), load(hx.at[0, 0], hw.at[1]), load(hy.at[0, 0], hw.at[2]),
        load(hp.at[0], hw.at[3]),
    ]
    get_z = load(mf.at[0, 0, 0], zf)
    get_c = load(cp.at[0, 0, 0], cf)
    get_h = load(hl.at[0, 0, 0], h0)
    get_b = load(hf.at[0, 0, 0], bf)
    late = [
        load(ms.at[0, 0, 0], sm), load(hs.at[0, 0, 0], sh),
        load(dn.at[0], den), load(ids.at[0], mat),
    ]

    barrier = pltpu.get_barrier_semaphore()
    for peer in y_peers + x_peers:
        pl.semaphore_signal(barrier, inc=1, device_id=peer, device_id_type=MESH)

    for d, there in enumerate(gets[:4]):
        @pl.when(jnp.logical_not(there))
        def _():
            qn[d] = jnp.zeros_like(qn[d])
            wn[d] = jnp.zeros_like(wn[d])
            hun[d] = jnp.zeros_like(hun[d])
            vn[d] = jnp.zeros_like(vn[d])
            bsn[d] = jnp.zeros_like(bsn[d])
    for d, there in ((0, high_x), (1, high_y)):
        @pl.when(jnp.logical_not(there))
        def _():
            mup[d] = jnp.zeros_like(mup[d])
            hup[d] = jnp.zeros_like(hup[d])
    col[...] = jnp.zeros_like(col)
    msc[...] = jnp.zeros_like(msc)

    def exchange(stage, src_of, dst):
        def copy(d):
            k = stage * 5 + d
            return remote(src_of(d), dst.at[d], esend.at[k], erecv.at[k], target[d])

        def start(order=(4, 0, 1, 2, 3)):
            for d in order:
                guarded(sends[d], lambda: copy(d).start())

        def arrive(order=(0, 1, 2, 3)):
            for d in order:
                guarded(gets[d], lambda: copy(d).wait_recv())

        def sent(order=(0, 1, 2, 3, 4)):
            for d in order:
                guarded(sends[d], lambda: copy(d).wait_send())

        return start, arrive, sent

    low, high = pl.ds(0, HALF), pl.ds(HALF, HALF)
    mine = pl.ds(pl.multiple_of(f * HALF, HALF), HALF)
    yours = pl.ds(pl.multiple_of((1 - f) * HALF, HALF), HALF)
    half = (low, high, low, high, yours)
    q_start, q_arrive, q_sent = exchange(0, lambda d: q0, qn)
    hu_start, hu_arrive, hu_sent = exchange(1, lambda d: hu, hun)
    w_start, w_arrive, w_sent = exchange(2, lambda d: wb.at[half[d]], wn)
    v_start, v_arrive, v_sent = exchange(3, lambda d: vb, vn)
    b_start, b_arrive, b_sent = exchange(4, lambda d: bsb.at[half[d]], bsn)

    get_r0.wait()
    q0[...] = r0[...].astype(BF16)
    pl.semaphore_wait(barrier, len(x_peers) + len(y_peers))
    q_start()
    for copy in small:
        copy.wait()

    def weights(k):
        src, dst, peer = (
            (mw.at[1], mup.at[0], down_x), (mw.at[2], mup.at[1], down_y),
            (hw.at[1], hup.at[0], down_x), (hw.at[2], hup.at[1], down_y),
        )[k]
        return remote(src, dst, wsend.at[k], wrecv.at[k], peer)

    for k in range(4):
        guarded((low_x, low_y)[k % 2], lambda: weights(k).start())

    get_z.wait()
    inner = times(q0[...], zf[...]).astype(BF16)
    w0[...] = times_t(inner, zf[...])
    get_c.wait()
    uf[...] = times(q0[...], cf[...])
    get_h.wait()
    hu[:, :256] = h0[...].astype(BF16)
    hu[:, 256:] = uf[...].astype(BF16)
    get_b.wait()
    for n in range(2):
        cols = slice(256 * n, 256 * n + 256)
        inner = times(hu[:, cols], bf[...]).astype(BF16)
        bhu[:, cols] = times_t(inner, bf[...])
    for k in range(4):
        guarded((high_x, high_y)[k % 2], lambda: weights(k).wait_recv())

    def near(part, w, up, values, nb, rows, cols=slice(None)):
        diag, wx, wy, wp = w[0], w[1], w[2], w[3]
        ux, uy = up[0], up[1]
        total = part + (diag + wx + ux + wy + uy + wp) * values
        total = total - wx * nb[0, rows, cols].astype(F32) - ux * nb[1, rows, cols].astype(F32)
        return total - wy * nb[2, rows, cols].astype(F32) - uy * nb[3, rows, cols].astype(F32)

    q_arrive()

    def body(rows):
        w0[rows, :] = near(w0[rows, :], mw, mup, q0[rows, :].astype(F32), qn, rows)

    row_loop(body)
    q_sent((4,))
    hu_start()
    q_arrive((4,))

    def body(rows):
        w = w0[rows, :] - mw[3] * qn[4, rows, :].astype(F32)
        w0[rows, :] = w
        wb[rows, :] = w.astype(BF16)

    row_loop(body)
    w_start()
    vf[...] = times(wb[...], cf[...])
    vb[...] = vf[...].astype(BF16)
    v_start()

    def moments(r, w, b, first, edge, inner, weight, up):
        def body(rows):
            rv, wv, bv_ = r[rows, :], w[rows, :], b[rows, :].astype(F32)
            col[rows, 0:1] = lanes(rv * rv)
            col[rows, 1:2] = lanes(rv * wv)
            col[rows, 2:3] = lanes(wv * wv)
            col[rows, 3:4] = lanes(bv_ * wv)
            col[rows, 4:5] = lanes(weight[0] * bv_ * bv_) + lanes(inner[rows, :] * inner[rows, :])

        row_loop(body)

    def edges(b, nb, weight, up):
        ends = jnp.where(low_x, 0.0, weight[1]) + jnp.where(low_y, 0.0, weight[2])

        def body(n, carry):
            rows = pl.ds(pl.multiple_of(n * ROWS, ROWS), ROWS)
            bv_ = b[rows, :].astype(F32)
            dx, dy = bv_ - nb[0, rows, :].astype(F32), bv_ - nb[2, rows, :].astype(F32)
            col[rows, 4:5] += lanes(weight[1] * dx * dx + weight[2] * dy * dy)
            upper = pl.ds(pl.multiple_of(HALF + n * ROWS, ROWS), ROWS)
            bv_ = b[upper, :].astype(F32)
            dx, dy = bv_ - nb[1, rows, :].astype(F32), bv_ - nb[3, rows, :].astype(F32)
            col[upper, 4:5] += lanes(up[0] * dx * dx + up[1] * dy * dy + ends * bv_ * bv_)
            return carry

        lax.fori_loop(0, HALF // ROWS, body, 0)

    def face_edges(b, nb, weight):
        def body(n, carry):
            rows = pl.ds(pl.multiple_of(n * ROWS, ROWS), ROWS)
            own = pl.ds(pl.multiple_of(f * HALF + n * ROWS, ROWS), ROWS)
            d = b[own, :].astype(F32) - nb[4, rows, :].astype(F32)
            col[own, 4:5] += lanes(weight[3] * d * d)
            return carry

        lax.fori_loop(0, HALF // ROWS, body, 0)

    def sum_start(buf, slot, peers, k):
        for peer in peers:
            remote(mom.at[k], buf.at[slot], asend.at[k], arecv.at[k], peer).start()
        buf[slot] = mom[k]

    def sum_end(buf, k):
        rest = buf.at[pl.ds(0, buf.shape[0] - 1)]
        pltpu.make_async_copy(rest, rest, arecv.at[k]).wait()
        return jnp.sum(buf[...], axis=0)

    def sum_sent(buf, k):
        rest = buf.at[pl.ds(0, buf.shape[0] - 1)]
        pltpu.make_async_copy(rest, rest, asend.at[k]).wait()

    xm[...] = times(wb[...], zf[...])
    moments(r0, w0, wb, None, None, xm, mw, mup)
    w_arrive()
    edges(wb, wn, mw, mup)
    w_arrive((4,))
    face_edges(wb, wn, mw)
    mom[0] = jnp.transpose(col[...])[:8, :]
    sum_start(arx1, x_slot, x_peers, 0)

    hu_arrive((0, 1, 2, 3, 4))

    def body(rows):
        for n in range(2):
            cols = slice(256 * n, 256 * n + 256)
            near_part = near(
                bhu[rows, cols], hw, hup, hu[rows, cols].astype(F32), hun, rows, cols
            )
            bhu[rows, cols] = near_part - hw[3] * hun[4, rows, cols].astype(F32)

    row_loop(body)
    mom[1] = sum_end(arx1, 0)
    sum_start(ary1, y_slot, y_peers, 1)
    inner = times(vb[...], bf[...]).astype(BF16)
    bv[...] = times_t(inner, bf[...])
    v_arrive((0, 1, 2, 3, 4))

    def body(rows):
        near_part = near(bv[rows, :], hw, hup, vb[rows, :].astype(F32), vn, rows)
        bv[rows, :] = near_part - hw[3] * vn[4, rows, :].astype(F32)

    row_loop(body)

    def columns(pair, k):
        msc[0:1, :] = pair[0]
        msc[1:2, :] = pair[1]
        col[...] = jnp.transpose(msc[...])

    total = sum_end(ary1, 1)
    columns(step_sizes(total), 0)

    def body(rows):
        a, b = col[rows, 0:1], col[rows, 1:2]
        s0[rows, :] = h0[rows, :] - a * uf[rows, :] - b * vf[rows, :]
        image = bhu[rows, :256] - a * bhu[rows, 256:] - b * bv[rows, :]
        bs[rows, :] = image
        bsb[rows, :] = image.astype(BF16)

    row_loop(body)
    b_start()

    def body(n, energy):
        rows = pl.ds(pl.multiple_of(n * ROWS, ROWS), ROWS)
        x = col[rows, 0:1] * r0[rows, :] + col[rows, 1:2] * w0[rows, :]
        xm[rows, :] = x
        return energy + jnp.sum(x * x, axis=0, keepdims=True)

    m_energy = lax.fori_loop(0, LOADS // ROWS, body, jnp.zeros((1, r0.shape[1]), F32))
    put_m = pltpu.make_async_copy(xm, out_m.at[0, 0, 0], osem.at[0])
    put_m.start()

    xh[...] = times(bsb[...], bf[...])
    moments(s0, bs, bsb, None, None, xh, hw, hup)
    b_arrive()
    edges(bsb, bsn, hw, hup)
    b_arrive((4,))
    face_edges(bsb, bsn, hw)
    mom[2] = jnp.transpose(col[...])[:8, :]
    sum_start(arx2, x_slot, x_peers, 2)
    for copy in late:
        copy.wait()
    wide = jnp.broadcast_to(m_energy.astype(BF16), (16, m_energy.shape[1]))
    sens = times(wide, sm[...])
    mom[3] = sum_end(arx2, 2)
    sum_start(ary2, y_slot, y_peers, 3)
    total = sum_end(ary2, 3)
    columns(step_sizes(total), 1)

    def body(n, energy):
        rows = pl.ds(pl.multiple_of(n * ROWS, ROWS), ROWS)
        x = col[rows, 0:1] * s0[rows, :] + col[rows, 1:2] * bs[rows, :]
        xh[rows, :] = x
        return energy + jnp.sum(x * x, axis=0, keepdims=True)

    h_energy = lax.fori_loop(0, LOADS // ROWS, body, jnp.zeros((1, h0.shape[1]), F32))
    put_h = pltpu.make_async_copy(xh, out_h.at[0, 0, 0], osem.at[1])
    put_h.start()
    wide = jnp.broadcast_to(h_energy.astype(BF16), (16, h_energy.shape[1]))
    sens = sens + times(wide, sh[...])
    sp[0] = sens[:8, :128]
    sp[1] = sens[:8, 128:]
    swap = remote(sp.at[1 - f], sr, fsem.at[0], fsem.at[1], other)
    swap.start()
    kinds = mat[...]
    stiffness = jnp.zeros(kinds.shape, F32)
    for k in range(scale.shape[0]):
        stiffness = jnp.where(kinds == k, scale[k], stiffness)
    factor = -3.0 * den[...] * den[...] * stiffness / LOADS
    swap.wait()
    out_g[0] = factor * (sp[f, 0:1, :] + sr[0:1, :])

    for k in range(4):
        guarded((low_x, low_y)[k % 2], lambda: weights(k).wait_send())
    q_sent((0, 1, 2, 3))
    for sent in (hu_sent, w_sent, v_sent, b_sent):
        sent()
    for k, buf in enumerate((arx1, ary1, arx2, ary2)):
        sum_sent(buf, k)
    put_m.wait()
    put_h.wait()


def solution(mesh):
    nx, ny = mesh.shape["gx"], mesh.shape["gy"]
    zs = 8 if nx % 8 == 0 else 1
    xs = nx // zs

    def vm(*shape, dtype=F32):
        return pltpu.VMEM(shape, dtype)

    def bm(*shape):
        return pltpu.VMEM(shape, BF16)

    any_spec = pl.BlockSpec(memory_space=pltpu.HBM)
    sems = pltpu.SemaphoreType.DMA

    def on_device(*args):
        return pl.pallas_call(
            functools.partial(kernel, nx, ny, xs, zs),
            out_shape=(
                jax.ShapeDtypeStruct((1, 1, 1, 128, 768), F32),
                jax.ShapeDtypeStruct((1, 1, 1, 128, 256), F32),
                jax.ShapeDtypeStruct((1, 1, 128), F32),
            ),
            in_specs=[any_spec] * 17 + [pl.BlockSpec(memory_space=pltpu.SMEM)],
            out_specs=(any_spec, any_spec, pl.BlockSpec(memory_space=pltpu.VMEM)),
            scratch_shapes=[
                vm(128, 768), vm(128, 256), bm(768, 768), bm(256, 256),
                vm(4, 1, 768), vm(4, 1, 256), vm(2, 1, 768), vm(2, 1, 256),
                bm(768, 256), bm(768, 256), bm(256, 256), vm(1, 128), vm(1, 128, dtype=jnp.int32),
                bm(128, 768), bm(5, 128, 768), vm(128, 768), bm(128, 768), bm(5, 64, 768),
                bm(128, 512), bm(5, 128, 512), vm(128, 256), vm(128, 512),
                vm(128, 256), bm(128, 256), bm(5, 128, 256), vm(128, 256),
                vm(128, 256), vm(128, 256), bm(128, 256), bm(5, 64, 256),
                vm(128, 128), vm(128, 128), vm(4, 8, 128),
                vm(nx, 8, 128), vm(ny * 2, 8, 128), vm(nx, 8, 128), vm(ny * 2, 8, 128),
                vm(128, 768), vm(128, 256), vm(2, 8, 128), vm(8, 128),
                sems((17,)), sems((2,)), sems((4,)), sems((4,)), sems((25,)), sems((25,)),
                sems((4,)), sems((4,)), sems((2,)),
            ],
            compiler_params=pltpu.CompilerParams(
                collective_id=0, has_side_effects=True, vmem_limit_bytes=32 * 1024 * 1024
            ),
        )(*args)

    block = P("gx", "gy", "phys", None, None)
    line = P("gx", "gy", "phys", None)
    both = P("gx", "gy", None)
    part = P("gx", "gy", "phys")
    return jax.shard_map(
        on_device,
        mesh=mesh,
        in_specs=(
            block, block, block, block, line, line, line, line, both, line, line, both,
            block, block, block, part, part, P(),
        ),
        out_specs=(block, block, part),
        check_vma=False,
    )
```

```python
import functools

import jax
import jax.numpy as jnp
from jax import lax
from jax.experimental import pallas as pl
from jax.experimental.pallas import tpu as pltpu
from jax.sharding import PartitionSpec as P

MESH = pl.DeviceIdType.MESH
F32 = jnp.float32
BF16 = jnp.bfloat16
ROWS = 16
LOADS = 128
HALF = LOADS // 2


def ring(k, n):
    return min(k, n - k)


def remote(src, dst, send, recv, peer):
    return pltpu.make_async_remote_copy(
        src_ref=src, dst_ref=dst, send_sem=send, recv_sem=recv, device_id=peer, device_id_type=MESH
    )


class Once:
    def __init__(self, wait, group):
        self.pending = wait
        group.append(self)

    def wait(self):
        if self.pending is not None:
            self.pending()
            self.pending = None


def row_loop(body, count=LOADS):
    def step(n, carry):
        body(pl.ds(pl.multiple_of(n * ROWS, ROWS), ROWS))
        return carry

    lax.fori_loop(0, count // ROWS, step, 0)


def lanes(x):
    return jnp.sum(x, axis=1, keepdims=True)


def times(a, b):
    return jnp.dot(a, b, preferred_element_type=F32)


def times_t(a, b):
    return lax.dot_general(a, b, (((1,), (1,)), ((), ())), preferred_element_type=F32)


def step_sizes(total):
    rr, rw, ww, gw, hw = (total[k : k + 1, :] for k in range(5))
    alpha = rr / rw
    beta = (rr - 2.0 * alpha * rw + alpha * alpha * ww) / rr
    grow = 1.0 + beta
    curve = grow * grow * rw - 2.0 * grow * alpha * gw + alpha * alpha * hw
    second = beta * rr / curve
    return alpha + second * grow, -second * alpha


def kernel(
    nx, ny, xs, zs,
    ml, hl, mf, hf, md, hd, mx, my, mp, hx, hy, hp, cp, ms, hs, dn, ids, sc,
    out_m, out_h, out_g,
    r0, h0, zf, bf, mw, hw, mup, hup, cf, sm, sh, shp, den, mat, scale,
    q0, qn, w0, wb, wn, hb, hn, bh, uv, uvb, uvn, buv, s0, sp, bs, bsb, bsn, bsp,
    msc, col, mom, arx1, ary1, arx2, ary2, xm, xh, part, got,
    lsem, wsend, wrecv, esend, erecv, asend, arecv, fsend, frecv,
):
    i, j, f = lax.axis_index("gx"), lax.axis_index("gy"), lax.axis_index("phys")
    low_x, high_x, low_y, high_y = i > 0, i < nx - 1, j > 0, j < ny - 1
    up_x = (jnp.minimum(i + 1, nx - 1), j, f)
    down_x = (jnp.maximum(i - 1, 0), j, f)
    up_y = (i, jnp.minimum(j + 1, ny - 1), f)
    down_y = (i, jnp.maximum(j - 1, 0), f)
    other = (i, j, 1 - f)
    target = (up_x, down_x, up_y, down_y, other)
    sends = (high_x, low_x, high_y, low_y, None)
    gets = (low_x, high_x, low_y, high_y, None)

    def guarded(cond, fn):
        if cond is None:
            fn()
        else:
            pl.when(cond)(fn)

    xi, zi = lax.div(i, zs), lax.rem(i, zs)
    offsets = [(a, b) for a in range(xs) for b in range(zs) if (a, b) != (0, 0)]
    offsets.sort(key=lambda o: -(ring(o[0], xs) + ring(o[1], zs)))
    x_peers = [(lax.rem(xi + a, xs) * zs + lax.rem(zi + b, zs), j, f) for a, b in offsets]
    yi, ci = f * (ny // 2) + lax.div(j, 2), lax.rem(j, 2)
    offsets = [(a, b) for a in range(ny) for b in range(2) if (a, b) != (0, 0)]
    offsets.sort(key=lambda o: -(ring(o[0], ny) + 0.1 * o[1]))
    y_peers = []
    for a, b in offsets:
        y = lax.rem(yi + a, ny)
        y_peers.append((i, lax.rem(y, ny // 2) * 2 + lax.rem(ci + b, 2), lax.div(y, ny // 2)))
    x_slot, y_slot = i, yi * 2 + ci

    finish = []

    def load(src, dst):
        copy = pltpu.make_async_copy(src, dst, lsem.at[len(finish)])
        copy.start()
        return Once(copy.wait, finish)

    def close():
        for piece in finish:
            piece.wait()

    get_r0 = load(ml.at[0, 0, 0], r0)
    barrier = pltpu.get_barrier_semaphore()
    for peer in y_peers + x_peers:
        pl.semaphore_signal(barrier, inc=1, device_id=peer, device_id_type=MESH)

    for d, there in enumerate(gets[:4]):
        @pl.when(jnp.logical_not(there))
        def _():
            for ref in (qn, wn, hn, uvn, bsn):
                ref[d] = jnp.zeros_like(ref[d])
    for d, there in ((0, high_x), (1, high_y)):
        @pl.when(jnp.logical_not(there))
        def _():
            mup[d] = jnp.zeros_like(mup[d])
            hup[d] = jnp.zeros_like(hup[d])

    def exchange(stage, src_of, dst_of):
        receipts, departures = {}, {}

        def copy(d):
            k = stage * 5 + d
            return remote(src_of(d), dst_of(d), esend.at[k], erecv.at[k], target[d])

        def start(order=(4, 0, 1, 2, 3)):
            for d in order:
                guarded(sends[d], lambda: copy(d).start())
                receipts[d] = Once(lambda d=d: guarded(gets[d], copy(d).wait_recv), finish)
                departures[d] = Once(lambda d=d: guarded(sends[d], copy(d).wait_send), finish)

        def arrive(order=(0, 1, 2, 3)):
            for d in order:
                receipts[d].wait()

        def sent(order):
            for d in order:
                departures[d].wait()

        return start, arrive, sent

    low, high = pl.ds(0, HALF), pl.ds(HALF, HALF)
    mine = pl.ds(pl.multiple_of(f * HALF, HALF), HALF)
    yours = pl.ds(pl.multiple_of((1 - f) * HALF, HALF), HALF)
    half = (low, high, low, high, yours)
    q_start, q_arrive, q_sent = exchange(0, lambda d: q0, lambda d: qn.at[d])
    h_start, h_arrive, h_sent = exchange(1, lambda d: hb, lambda d: hn.at[d])
    w_start, w_arrive, w_sent = exchange(2, lambda d: wb.at[half[d]], lambda d: wn.at[d])
    uv_start, uv_arrive, uv_sent = exchange(3, lambda d: uvb, lambda d: uvn.at[d])
    b_start, b_arrive, b_sent = exchange(
        4, lambda d: bsb.at[half[d]], lambda d: bsp.at[yours] if d == 4 else bsn.at[d]
    )

    def face_send(k, src, dst):
        copy = remote(src, dst, fsend.at[k], frecv.at[k], other)
        copy.start()
        Once(copy.wait_send, finish)
        return Once(copy.wait_recv, finish)

    get_r0.wait()
    q0[...] = r0[...].astype(BF16)
    pl.semaphore_wait(barrier, len(x_peers) + len(y_peers))
    q_start()
    small = [
        load(md.at[0, 0], mw.at[0]), load(mx.at[0, 0], mw.at[1]), load(my.at[0, 0], mw.at[2]),
        load(mp.at[0], mw.at[3]),
        load(hd.at[0, 0], hw.at[0]), load(hx.at[0, 0], hw.at[1]), load(hy.at[0, 0], hw.at[2]),
        load(hp.at[0], hw.at[3]),
    ]
    get_z = load(mf.at[0, 0, 0], zf)
    get_c = load(cp.at[0, 0, 0], cf)
    get_h = load(hl.at[0, 0, 0], h0)
    get_b = load(hf.at[0, 0, 0], bf)
    get_sm = load(ms.at[0, 0, 0], sm)
    get_sh = [load(hs.at[0, 0, 0, :, pl.ds(128 * k, 128)], sh.at[k]) for k in range(2)]
    get_last = [load(dn.at[0], den), load(ids.at[0], mat), load(sc, scale)]
    for copy in small:
        copy.wait()

    def weights(k):
        src, dst, peer = (
            (mw.at[1], mup.at[0], down_x), (mw.at[2], mup.at[1], down_y),
            (hw.at[1], hup.at[0], down_x), (hw.at[2], hup.at[1], down_y),
        )[k]
        return remote(src, dst, wsend.at[k], wrecv.at[k], peer)

    above = []
    for k in range(4):
        guarded((low_x, low_y)[k % 2], lambda: weights(k).start())
        Once(lambda k=k: guarded((low_x, low_y)[k % 2], lambda: weights(k).wait_send()), finish)
        above.append(
            Once(lambda k=k: guarded((high_x, high_y)[k % 2], lambda: weights(k).wait_recv()), finish)
        )
    col[...] = jnp.zeros_like(col)
    msc[...] = jnp.zeros_like(msc)

    get_z.wait()
    inner = times(q0[...], zf[...]).astype(BF16)
    w0[...] = times_t(inner, zf[...])
    get_c.wait()
    uv[:, :256] = times(q0[...], cf[...])
    get_h.wait()
    hb[...] = h0[...].astype(BF16)
    get_b.wait()
    bh[...] = times_t(times(hb[...], bf[...]).astype(BF16), bf[...])
    for copy in above:
        copy.wait()

    def near(total, w, up, values, nb, rows, cols=slice(None)):
        diag, wx, wy, wp = w[0], w[1], w[2], w[3]
        ux, uy = up[0], up[1]
        total = total + (diag + wx + ux + wy + uy + wp) * values
        total = total - wx * nb[0, rows, cols].astype(F32) - ux * nb[1, rows, cols].astype(F32)
        return total - wy * nb[2, rows, cols].astype(F32) - uy * nb[3, rows, cols].astype(F32)

    q_arrive()

    def body(rows):
        w0[rows, :] = near(w0[rows, :], mw, mup, q0[rows, :].astype(F32), qn, rows)

    row_loop(body)
    q_sent((4,))
    h_start()
    q_arrive((4,))

    def body(rows):
        w = w0[rows, :] - mw[3] * qn[4, rows, :].astype(F32)
        w0[rows, :] = w
        wb[rows, :] = w.astype(BF16)

    row_loop(body)
    w_start()
    uv[:, 256:] = times(wb[...], cf[...])
    uvb[...] = uv[...].astype(BF16)

    def moments(r, w, b, inner, weight):
        def body(rows):
            rv, wv, bv = r[rows, :], w[rows, :], b[rows, :].astype(F32)
            col[rows, 0:1] = lanes(rv * rv)
            col[rows, 1:2] = lanes(rv * wv)
            col[rows, 2:3] = lanes(wv * wv)
            col[rows, 3:4] = lanes(bv * wv)
            col[rows, 4:5] = lanes(weight[0] * bv * bv) + lanes(inner[rows, :] * inner[rows, :])

        row_loop(body)

    def edges(b, nb, weight, up):
        ends = jnp.where(low_x, 0.0, weight[1]) + jnp.where(low_y, 0.0, weight[2])

        def body(rows):
            bv = b[rows, :].astype(F32)
            dx, dy = bv - nb[0, rows, :].astype(F32), bv - nb[2, rows, :].astype(F32)
            col[rows, 4:5] += lanes(weight[1] * dx * dx + weight[2] * dy * dy)

        row_loop(body, HALF)

        def body(n, carry):
            rows = pl.ds(pl.multiple_of(n * ROWS, ROWS), ROWS)
            upper = pl.ds(pl.multiple_of(HALF + n * ROWS, ROWS), ROWS)
            bv = b[upper, :].astype(F32)
            dx, dy = bv - nb[1, rows, :].astype(F32), bv - nb[3, rows, :].astype(F32)
            col[upper, 4:5] += lanes(up[0] * dx * dx + up[1] * dy * dy + ends * bv * bv)
            return carry

        lax.fori_loop(0, HALF // ROWS, body, 0)

    def face_edges(b, there, weight):
        def body(n, carry):
            rows = pl.ds(pl.multiple_of(n * ROWS, ROWS), ROWS)
            own = pl.ds(pl.multiple_of(f * HALF + n * ROWS, ROWS), ROWS)
            d = b[own, :].astype(F32) - there(rows, own).astype(F32)
            col[own, 4:5] += lanes(weight[3] * d * d)
            return carry

        lax.fori_loop(0, HALF // ROWS, body, 0)

    def sum_start(buf, slot, peers, k):
        for peer in peers:
            remote(mom.at[k], buf.at[slot], asend.at[k], arecv.at[k], peer).start()
        buf[slot] = mom[k]
        rest = buf.at[pl.ds(0, buf.shape[0] - 1)]
        arrived = Once(lambda: pltpu.make_async_copy(rest, rest, arecv.at[k]).wait(), finish)
        Once(lambda: pltpu.make_async_copy(rest, rest, asend.at[k]).wait(), finish)

        def end():
            arrived.wait()
            return jnp.sum(buf[...], axis=0)

        return end

    xm[...] = times(wb[...], zf[...])
    moments(r0, w0, wb, xm, mw)
    w_sent((4,))
    uv_start()
    w_arrive()
    edges(wb, wn, mw, mup)
    w_arrive((4,))
    face_edges(wb, lambda rows, own: wn[4, rows, :], mw)
    mom[0] = jnp.transpose(col[...])[:8, :]
    sum_arx1 = sum_start(arx1, x_slot, x_peers, 0)

    for k in range(2):
        cols = slice(256 * k, 256 * k + 256)
        buv[:, cols] = times_t(times(uvb[:, cols], bf[...]).astype(BF16), bf[...])
    h_arrive((0, 1, 2, 3, 4))

    def body(rows):
        total = near(bh[rows, :], hw, hup, hb[rows, :].astype(F32), hn, rows)
        bh[rows, :] = total - hw[3] * hn[4, rows, :].astype(F32)

    row_loop(body)
    mom[1] = sum_arx1()
    sum_ary1 = sum_start(ary1, y_slot, y_peers, 1)
    uv_arrive((0, 1, 2, 3, 4))

    def body(rows):
        for k in range(2):
            cols = slice(256 * k, 256 * k + 256)
            total = near(buv[rows, cols], hw, hup, uvb[rows, cols].astype(F32), uvn, rows, cols)
            buv[rows, cols] = total - hw[3] * uvn[4, rows, cols].astype(F32)

    row_loop(body)

    def columns(pair):
        msc[0:1, :] = pair[0]
        msc[1:2, :] = pair[1]
        col[...] = jnp.transpose(msc[...])

    total = sum_ary1()
    columns(step_sizes(total))

    def body(rows):
        a, b = col[rows, 0:1], col[rows, 1:2]
        image = bh[rows, :] - a * buv[rows, :256] - b * buv[rows, 256:]
        bs[rows, :] = image
        bsb[rows, :] = image.astype(BF16)

    row_loop(body)
    b_start()
    get_b2 = face_send(0, bsb.at[mine], bsp.at[mine])
    for copy in get_sh:
        copy.wait()
    get_shp = face_send(1, sh.at[1 - f], shp)

    def body(n, energy):
        rows = pl.ds(pl.multiple_of(n * ROWS, ROWS), ROWS)
        a, b = col[rows, 0:1], col[rows, 1:2]
        s0[rows, :] = h0[rows, :] - a * uv[rows, :256] - b * uv[rows, 256:]
        sp[rows, :] = (
            hn[4, rows, :].astype(F32)
            - a * uvn[4, rows, :256].astype(F32)
            - b * uvn[4, rows, 256:].astype(F32)
        )
        x = a * r0[rows, :] + b * w0[rows, :]
        out_m[0, 0, 0, rows, :] = x
        return energy + jnp.sum(x * x, axis=0, keepdims=True)

    energy = lax.fori_loop(0, LOADS // ROWS, body, jnp.zeros((1, r0.shape[1]), F32))
    get_sm.wait()
    sens = times(jnp.broadcast_to(energy.astype(BF16), (16, energy.shape[1])), sm[...])
    part[0] = sens[:8, :128]
    part[1] = sens[:8, 128:]
    get_part = face_send(2, part.at[1 - f], got)
    xh[...] = times(bsb[...], bf[...])
    moments(s0, bs, bsb, xh, hw)
    b_arrive()
    edges(bsb, bsn, hw, hup)
    b_arrive((4,))
    face_edges(bsb, lambda rows, own: bsp[own, :], hw)
    mom[2] = jnp.transpose(col[...])[:8, :]
    sum_arx2 = sum_start(arx2, x_slot, x_peers, 2)
    for copy in get_last:
        copy.wait()
    kinds = mat[...]
    stiffness = jnp.zeros(kinds.shape, F32)
    for k in range(scale.shape[0]):
        stiffness = jnp.where(kinds == k, scale[k], stiffness)
    factor = -3.0 * den[...] * den[...] * stiffness / LOADS
    get_b2.wait()
    get_part.wait()
    get_shp.wait()
    sens = part[f, 0:1, :] + got[0:1, :]
    mom[3] = sum_arx2()
    sum_ary2 = sum_start(ary2, y_slot, y_peers, 3)
    total = sum_ary2()
    columns(step_sizes(total))

    def body(n, energies):
        rows = pl.ds(pl.multiple_of(n * ROWS, ROWS), ROWS)
        a, b = col[rows, 0:1], col[rows, 1:2]
        x = a * s0[rows, :] + b * bs[rows, :]
        out_h[0, 0, 0, rows, :] = x
        there = a * sp[rows, :] + b * bsp[rows, :].astype(F32)
        return (
            energies[0] + jnp.sum(x * x, axis=0, keepdims=True),
            energies[1] + jnp.sum(there * there, axis=0, keepdims=True),
        )

    zero = jnp.zeros((1, h0.shape[1]), F32)
    energies = lax.fori_loop(0, LOADS // ROWS, body, (zero, zero))
    for energy, table in zip(energies, (sh[f], shp[...])):
        wide = jnp.broadcast_to(energy.astype(BF16), (16, energy.shape[1]))
        sens = sens + times(wide, table)[0:1, :]
    out_g[0] = factor * sens
    close()


def place(a, b, c, x, y, z, sem):
    copies = [
        pltpu.make_async_copy(src, dst, sem.at[k])
        for k, (src, dst) in enumerate(((a, x), (b, y), (c, z)))
    ]
    for copy in copies:
        copy.start()
    for copy in copies:
        copy.wait()


def solution(mesh):
    nx, ny = mesh.shape["gx"], mesh.shape["gy"]
    zs = 8 if nx % 8 == 0 else 1
    xs = nx // zs

    def vm(*shape, dtype=F32):
        return pltpu.VMEM(shape, dtype)

    def bm(*shape):
        return pltpu.VMEM(shape, BF16)

    in_hbm = pl.BlockSpec(memory_space=pltpu.HBM)
    in_vmem = pl.BlockSpec(memory_space=pltpu.VMEM)
    sems = pltpu.SemaphoreType.DMA
    outs = (
        jax.ShapeDtypeStruct((1, 1, 1, 128, 768), F32),
        jax.ShapeDtypeStruct((1, 1, 1, 128, 256), F32),
        jax.ShapeDtypeStruct((1, 1, 128), F32),
    )

    def on_device(*args):
        results = pl.pallas_call(
            functools.partial(kernel, nx, ny, xs, zs),
            out_shape=outs,
            in_specs=[in_hbm] * 18,
            out_specs=(in_vmem,) * 3,
            scratch_shapes=[
                vm(128, 768), vm(128, 256), bm(768, 768), bm(256, 256),
                vm(4, 1, 768), vm(4, 1, 256), vm(2, 1, 768), vm(2, 1, 256),
                bm(768, 256), bm(768, 256), bm(2, 256, 128), bm(256, 128),
                vm(1, 128), vm(1, 128, dtype=jnp.int32), pltpu.SMEM((8,), F32),
                bm(128, 768), bm(5, 128, 768), vm(128, 768), bm(128, 768), bm(5, 64, 768),
                bm(128, 256), bm(5, 128, 256), vm(128, 256),
                vm(128, 512), bm(128, 512), bm(5, 128, 512), vm(128, 512),
                vm(128, 256), vm(128, 256), vm(128, 256), bm(128, 256), bm(4, 64, 256),
                bm(128, 256),
                vm(128, 128), vm(128, 128), vm(4, 8, 128),
                vm(nx, 8, 128), vm(ny * 2, 8, 128), vm(nx, 8, 128), vm(ny * 2, 8, 128),
                vm(128, 768), vm(128, 256), vm(2, 8, 128), vm(8, 128),
                sems((64,)), sems((4,)), sems((4,)), sems((25,)), sems((25,)),
                sems((4,)), sems((4,)), sems((3,)), sems((3,)),
            ],
            compiler_params=pltpu.CompilerParams(
                collective_id=0, has_side_effects=True, vmem_limit_bytes=32 * 1024 * 1024
            ),
        )(*(pltpu.with_memory_space_constraint(a, pltpu.HBM) for a in args))
        return pl.pallas_call(
            place,
            out_shape=outs,
            in_specs=[in_vmem] * 3,
            out_specs=[in_hbm] * 3,
            scratch_shapes=[sems((3,))],
        )(*(pltpu.with_memory_space_constraint(a, pltpu.VMEM) for a in results))

    block = P("gx", "gy", "phys", None, None)
    line = P("gx", "gy", "phys", None)
    both = P("gx", "gy", None)
    part = P("gx", "gy", "phys")
    return jax.shard_map(
        on_device,
        mesh=mesh,
        in_specs=(
            block, block, block, block, line, line, line, line, both, line, line, both,
            block, block, block, part, part, P(),
        ),
        out_specs=(block, block, part),
        check_vma=False,
    )
```

```python
import functools

import jax
import jax.numpy as jnp
from jax import lax
from jax.experimental import pallas as pl
from jax.experimental.pallas import tpu as pltpu
from jax.sharding import PartitionSpec as P

MESH = pl.DeviceIdType.MESH
F32 = jnp.float32
BF16 = jnp.bfloat16
ROWS = 16
LOADS = 128
HALF = LOADS // 2
QUARTER = LOADS // 4


def ring(k, n):
    return min(k, n - k)


def remote(src, dst, send, recv, peer):
    return pltpu.make_async_remote_copy(
        src_ref=src, dst_ref=dst, send_sem=send, recv_sem=recv, device_id=peer, device_id_type=MESH
    )


class Once:
    def __init__(self, wait, group):
        self.pending = wait
        group.append(self)

    def wait(self):
        if self.pending is not None:
            self.pending()
            self.pending = None


def row_loop(body, count=LOADS, first=0):
    def step(n, carry):
        body(pl.ds(pl.multiple_of(first + n * ROWS, ROWS), ROWS))
        return carry

    lax.fori_loop(0, count // ROWS, step, 0)


def fold(x):
    return sum(x[:, k : k + 128] for k in range(0, x.shape[1], 128))


def lane_sums(parts):
    return lax.dot_general(
        jnp.ones((8, 128), F32), parts, (((1,), (1,)), ((), ())),
        precision=lax.Precision.HIGHEST, preferred_element_type=F32,
    )


def times(a, b):
    return jnp.dot(a, b, preferred_element_type=F32)


def times_t(a, b):
    return lax.dot_general(a, b, (((1,), (1,)), ((), ())), preferred_element_type=F32)


def step_sizes(total):
    rr, rw, ww, gw, hw = (total[k : k + 1, :] for k in range(5))
    alpha = rr / rw
    beta = (rr - 2.0 * alpha * rw + alpha * alpha * ww) / rr
    grow = 1.0 + beta
    curve = grow * grow * rw - 2.0 * grow * alpha * gw + alpha * alpha * hw
    second = beta * rr / curve
    return alpha + second * grow, -second * alpha


def kernel(
    nx, ny, xs, zs,
    ml, hl, mf, hf, md, hd, mx, my, mp, hx, hy, hp, cp, ms, hs, dn, ids, sc,
    out_m, out_h, out_g,
    r0, h0, zf, bf, mw, hw, mup, hup, cf, sm, sh, shp, den, mat, scale,
    q0, qn, w0, wb, wn, hb, hn, bh, uv, uvb, uvn, buv, s0, sp, bs, bsb, bsn, bsp,
    msc, col, pm, mom, arx1, ary1, arx2, ary2, xm, xh, part, got,
    lsem, wsend, wrecv, esend, erecv, asend, arecv, fsend, frecv,
):
    i, j, f = lax.axis_index("gx"), lax.axis_index("gy"), lax.axis_index("phys")
    low_x, high_x, low_y, high_y = i > 0, i < nx - 1, j > 0, j < ny - 1
    up_x = (jnp.minimum(i + 1, nx - 1), j, f)
    down_x = (jnp.maximum(i - 1, 0), j, f)
    up_y = (i, jnp.minimum(j + 1, ny - 1), f)
    down_y = (i, jnp.maximum(j - 1, 0), f)
    other = (i, j, 1 - f)
    target = (up_x, down_x, up_y, down_y, other)
    sends = (high_x, low_x, high_y, low_y, None)
    gets = (low_x, high_x, low_y, high_y, None)

    def guarded(cond, fn):
        if cond is None:
            fn()
        else:
            pl.when(cond)(fn)

    xi, zi = lax.div(i, zs), lax.rem(i, zs)
    offsets = [(a, b) for a in range(xs) for b in range(zs) if (a, b) != (0, 0)]
    offsets.sort(key=lambda o: -(ring(o[0], xs) + ring(o[1], zs)))
    x_peers = [(lax.rem(xi + a, xs) * zs + lax.rem(zi + b, zs), j, f) for a, b in offsets]
    yi, ci = f * (ny // 2) + lax.div(j, 2), lax.rem(j, 2)
    offsets = [(a, b) for a in range(ny) for b in range(2) if (a, b) != (0, 0)]
    offsets.sort(key=lambda o: -(ring(o[0], ny) + 0.1 * o[1]))
    y_peers = []
    for a, b in offsets:
        y = lax.rem(yi + a, ny)
        y_peers.append((i, lax.rem(y, ny // 2) * 2 + lax.rem(ci + b, 2), lax.div(y, ny // 2)))
    x_slot, y_slot = i, yi * 2 + ci

    finish = []

    def load(src, dst):
        copy = pltpu.make_async_copy(src, dst, lsem.at[len(finish)])
        copy.start()
        return Once(copy.wait, finish)

    def close():
        for piece in finish:
            piece.wait()

    get_r0 = [load(ml.at[0, 0, 0, pl.ds(HALF * c, HALF)], r0.at[pl.ds(HALF * c, HALF)]) for c in range(2)]
    barrier = pltpu.get_barrier_semaphore()
    for peer in y_peers + x_peers:
        pl.semaphore_signal(barrier, inc=1, device_id=peer, device_id_type=MESH)

    for d, there in enumerate(gets[:4]):
        @pl.when(jnp.logical_not(there))
        def _():
            for ref in (qn, wn, hn, uvn, bsn):
                ref[d] = jnp.zeros_like(ref[d])
            uvn[5 + d] = jnp.zeros_like(uvn[d])
    for d, there in ((0, high_x), (1, high_y)):
        @pl.when(jnp.logical_not(there))
        def _():
            mup[d] = jnp.zeros_like(mup[d])
            hup[d] = jnp.zeros_like(hup[d])

    def exchange(stage, src_of, dst_of):
        receipts, departures = {}, {}

        def copy(d):
            k = stage * 5 + d
            return remote(src_of(d), dst_of(d), esend.at[k], erecv.at[k], target[d])

        def start(order=(4, 0, 1, 2, 3)):
            for d in order:
                guarded(sends[d], lambda: copy(d).start())
                receipts[d] = Once(lambda d=d: guarded(gets[d], copy(d).wait_recv), finish)
                departures[d] = Once(lambda d=d: guarded(sends[d], copy(d).wait_send), finish)

        def arrive(order=(0, 1, 2, 3)):
            for d in order:
                receipts[d].wait()

        def sent(order):
            for d in order:
                departures[d].wait()

        return start, arrive, sent

    low, high = pl.ds(0, HALF), pl.ds(HALF, HALF)
    mine = pl.ds(pl.multiple_of(f * HALF, HALF), HALF)
    yours = pl.ds(pl.multiple_of((1 - f) * HALF, HALF), HALF)
    half = (low, high, low, high, yours)
    chunks = [pl.ds(HALF * c, HALF) for c in range(2)]
    q_sends = [
        exchange(s, lambda d, c=c: q0.at[chunks[c]], lambda d, c=c: qn.at[d, chunks[c]])
        for c, s in enumerate((0, 6))
    ]

    def ends_of(d, c):
        shift = (0, QUARTER, 0, QUARTER, (1 - f) * QUARTER)[d]
        return pl.ds(pl.multiple_of(HALF * c + shift, QUARTER), QUARTER)

    w_sends = [
        exchange(
            s,
            lambda d, c=c: wb.at[ends_of(d, c)],
            lambda d, c=c: wn.at[d, pl.ds(QUARTER * c, QUARTER)],
        )
        for c, s in enumerate((2, 7))
    ]
    h_start, h_arrive, h_sent = exchange(1, lambda d: hb, lambda d: hn.at[d])
    u_start, u_arrive, u_sent = exchange(3, lambda d: uvb.at[0], lambda d: uvn.at[d])
    v_start, v_arrive, v_sent = exchange(5, lambda d: uvb.at[1], lambda d: uvn.at[5 + d])
    b_start, b_arrive, b_sent = exchange(
        4, lambda d: bsb.at[half[d]], lambda d: bsp.at[yours] if d == 4 else bsn.at[d]
    )

    def face_send(k, src, dst):
        copy = remote(src, dst, fsend.at[k], frecv.at[k], other)
        copy.start()
        Once(copy.wait_send, finish)
        return Once(copy.wait_recv, finish)

    for c, (start, _, _) in enumerate(q_sends):
        get_r0[c].wait()
        q0[chunks[c], :] = r0[chunks[c], :].astype(BF16)
        if c == 0:
            pl.semaphore_wait(barrier, len(x_peers) + len(y_peers))
        start()
    small = [
        load(md.at[0, 0], mw.at[0]), load(mx.at[0, 0], mw.at[1]), load(my.at[0, 0], mw.at[2]),
        load(mp.at[0], mw.at[3]),
        load(hd.at[0, 0], hw.at[0]), load(hx.at[0, 0], hw.at[1]), load(hy.at[0, 0], hw.at[2]),
        load(hp.at[0], hw.at[3]),
    ]
    get_z = load(mf.at[0, 0, 0], zf)
    get_c = load(cp.at[0, 0, 0], cf)
    get_h = load(hl.at[0, 0, 0], h0)
    get_b = load(hf.at[0, 0, 0], bf)
    get_sm = load(ms.at[0, 0, 0], sm)
    get_sh = [load(hs.at[0, 0, 0, :, pl.ds(128 * k, 128)], sh.at[k]) for k in range(2)]
    get_last = [load(dn.at[0], den), load(ids.at[0], mat), load(sc, scale)]
    for copy in small:
        copy.wait()

    def weights(k):
        src, dst, peer = (
            (mw.at[1], mup.at[0], down_x), (mw.at[2], mup.at[1], down_y),
            (hw.at[1], hup.at[0], down_x), (hw.at[2], hup.at[1], down_y),
        )[k]
        return remote(src, dst, wsend.at[k], wrecv.at[k], peer)

    above = []
    for k in range(4):
        guarded((low_x, low_y)[k % 2], lambda: weights(k).start())
        Once(lambda k=k: guarded((low_x, low_y)[k % 2], lambda: weights(k).wait_send()), finish)
        above.append(
            Once(lambda k=k: guarded((high_x, high_y)[k % 2], lambda: weights(k).wait_recv()), finish)
        )
    mom[...] = jnp.zeros_like(mom)
    msc[...] = jnp.zeros_like(msc)

    get_z.wait()
    inner = times(q0[...], zf[...]).astype(BF16)
    w0[...] = times_t(inner, zf[...])
    get_c.wait()
    uv[:, :256] = times(q0[...], cf[...])
    uvb[0] = uv[:, :256].astype(BF16)
    get_h.wait()
    hb[...] = h0[...].astype(BF16)
    get_b.wait()
    bh[...] = times_t(times(hb[...], bf[...]).astype(BF16), bf[...])
    for copy in above:
        copy.wait()

    def near(total, w, up, values, nb, rows, cols=slice(None)):
        diag, wx, wy, wp = w[0], w[1], w[2], w[3]
        ux, uy = up[0], up[1]
        total = total + (diag + wx + ux + wy + uy + wp) * values
        total = total - wx * nb[0, rows, cols].astype(F32) - ux * nb[1, rows, cols].astype(F32)
        return total - wy * nb[2, rows, cols].astype(F32) - uy * nb[3, rows, cols].astype(F32)

    for c in range(2):
        start, arrive, sent = q_sends[c]
        arrive()

        def body(rows):
            w0[rows, :] = near(w0[rows, :], mw, mup, q0[rows, :].astype(F32), qn, rows)

        row_loop(body, HALF, HALF * c)
        arrive((4,))

        def body(rows):
            w = w0[rows, :] - mw[3] * qn[4, rows, :].astype(F32)
            w0[rows, :] = w
            wb[rows, :] = w.astype(BF16)

        row_loop(body, HALF, HALF * c)
        if c == 0:
            q_sends[1][2]((4,))
        else:
            w_sends[0][2]((4,))
        w_sends[c][0]()
    u_start((0, 1))
    h_start((0, 1))
    uv[:, 256:] = times(wb[...], cf[...])
    uvb[1] = uv[:, 256:].astype(BF16)
    v_start((0, 1))

    def moments(k, r, w, b, inner, weight):
        def body(rows):
            rv, wv, bv = r[rows, :], w[rows, :], b[rows, :].astype(F32)
            iv = inner[rows, :]
            pm[0, rows, :] = fold(rv * rv)
            pm[1, rows, :] = fold(rv * wv)
            pm[2, rows, :] = fold(wv * wv)
            pm[3, rows, :] = fold(bv * wv)
            pm[4, rows, :] = fold(weight[0] * bv * bv + iv * iv)

        row_loop(body)
        sums = lane_sums(pm[:4].reshape(4 * LOADS, 128))
        for n in range(4):
            mom[k, n : n + 1, :] = sums[0:1, n * LOADS : (n + 1) * LOADS]

    def moments_end(k):
        mom[k, 4:5, :] = lane_sums(pm[4])[0:1, :]

    def edges(b, nb, weight, up, first, there, count):
        ends = jnp.where(low_x, 0.0, weight[1]) + jnp.where(low_y, 0.0, weight[2])

        def body(n, carry):
            rows = pl.ds(pl.multiple_of(there + n * ROWS, ROWS), ROWS)
            lower = pl.ds(pl.multiple_of(first + n * ROWS, ROWS), ROWS)
            bv = b[lower, :].astype(F32)
            dx, dy = bv - nb[0, rows, :].astype(F32), bv - nb[2, rows, :].astype(F32)
            pm[4, lower, :] += fold(weight[1] * dx * dx + weight[2] * dy * dy)
            upper = pl.ds(pl.multiple_of(first + count + n * ROWS, ROWS), ROWS)
            bv = b[upper, :].astype(F32)
            dx, dy = bv - nb[1, rows, :].astype(F32), bv - nb[3, rows, :].astype(F32)
            pm[4, upper, :] += fold(up[0] * dx * dx + up[1] * dy * dy + ends * bv * bv)
            return carry

        lax.fori_loop(0, count // ROWS, body, 0)

    def face_edges(b, other_face, weight, first, there, count):
        def body(n, carry):
            rows = pl.ds(pl.multiple_of(there + n * ROWS, ROWS), ROWS)
            own = pl.ds(pl.multiple_of(first + f * count + n * ROWS, ROWS), ROWS)
            d = b[own, :].astype(F32) - other_face(rows, own).astype(F32)
            pm[4, own, :] += fold(weight[3] * d * d)
            return carry

        lax.fori_loop(0, count // ROWS, body, 0)

    def sum_start(buf, slot, peers, k):
        for peer in peers:
            remote(mom.at[k], buf.at[slot], asend.at[k], arecv.at[k], peer).start()
        buf[slot] = mom[k]
        rest = buf.at[pl.ds(0, buf.shape[0] - 1)]
        arrived = Once(lambda: pltpu.make_async_copy(rest, rest, arecv.at[k]).wait(), finish)
        Once(lambda: pltpu.make_async_copy(rest, rest, asend.at[k]).wait(), finish)

        def end():
            arrived.wait()
            return jnp.sum(buf[...], axis=0)

        return end

    xm[...] = times(wb[...], zf[...])
    moments(0, r0, w0, wb, xm, mw)
    w_sends[1][2]((4,))
    h_start((4, 2, 3))
    u_start((4, 2, 3))
    for c in range(2):
        w_sends[c][1]()
        edges(wb, wn, mw, mup, HALF * c, QUARTER * c, QUARTER)
        w_sends[c][1]((4,))
        face_edges(wb, lambda rows, own: wn[4, rows, :], mw, HALF * c, QUARTER * c, QUARTER)
    moments_end(0)
    sum_arx1 = sum_start(arx1, x_slot, x_peers, 0)
    v_start((4, 2, 3))

    for k in range(2):
        cols = slice(256 * k, 256 * k + 256)
        buv[:, cols] = times_t(times(uvb[k], bf[...]).astype(BF16), bf[...])
    h_arrive((0, 1, 2, 3, 4))

    def body(rows):
        total = near(bh[rows, :], hw, hup, hb[rows, :].astype(F32), hn, rows)
        bh[rows, :] = total - hw[3] * hn[4, rows, :].astype(F32)

    row_loop(body)
    mom[1] = sum_arx1()
    sum_ary1 = sum_start(ary1, y_slot, y_peers, 1)
    u_arrive((0, 1, 2, 3, 4))
    v_arrive((0, 1, 2, 3, 4))

    def body(rows):
        for k in range(2):
            cols = slice(256 * k, 256 * k + 256)
            there = uvn.at[5 * k : 5 * k + 5]
            total = near(buv[rows, cols], hw, hup, uvb[k, rows, :].astype(F32), there, rows)
            buv[rows, cols] = total - hw[3] * there[4, rows, :].astype(F32)

    row_loop(body)

    def columns(pair):
        msc[0:1, :] = pair[0]
        msc[1:2, :] = pair[1]
        col[...] = jnp.transpose(msc[...])

    total = sum_ary1()
    columns(step_sizes(total))

    def body(rows):
        a, b = col[rows, 0:1], col[rows, 1:2]
        image = bh[rows, :] - a * buv[rows, :256] - b * buv[rows, 256:]
        bs[rows, :] = image
        bsb[rows, :] = image.astype(BF16)

    row_loop(body)
    b_start()

    def body(n, energy):
        rows = pl.ds(pl.multiple_of(n * ROWS, ROWS), ROWS)
        a, b = col[rows, 0:1], col[rows, 1:2]
        s0[rows, :] = h0[rows, :] - a * uv[rows, :256] - b * uv[rows, 256:]
        sp[rows, :] = (
            hn[4, rows, :].astype(F32)
            - a * uvn[4, rows, :].astype(F32)
            - b * uvn[9, rows, :].astype(F32)
        )
        x = a * r0[rows, :] + b * w0[rows, :]
        out_m[0, 0, 0, rows, :] = x
        return energy + jnp.sum(x * x, axis=0, keepdims=True)

    energy = lax.fori_loop(0, LOADS // ROWS, body, jnp.zeros((1, r0.shape[1]), F32))
    get_sm.wait()
    sens = times(jnp.broadcast_to(energy.astype(BF16), (16, energy.shape[1])), sm[...])
    part[0] = sens[:8, :128]
    part[1] = sens[:8, 128:]
    xh[...] = times(bsb[...], bf[...])
    moments(2, s0, bs, bsb, xh, hw)
    b_arrive()
    edges(bsb, bsn, hw, hup, 0, 0, HALF)
    b_arrive((4,))
    face_edges(bsb, lambda rows, own: bsp[own, :], hw, 0, 0, HALF)
    moments_end(2)
    sum_arx2 = sum_start(arx2, x_slot, x_peers, 2)
    get_b2 = face_send(0, bsb.at[mine], bsp.at[mine])
    get_part = face_send(2, part.at[1 - f], got)
    for copy in get_sh:
        copy.wait()
    get_shp = face_send(1, sh.at[1 - f], shp)
    for copy in get_last:
        copy.wait()
    kinds = mat[...]
    stiffness = jnp.zeros(kinds.shape, F32)
    for k in range(scale.shape[0]):
        stiffness = jnp.where(kinds == k, scale[k], stiffness)
    factor = -3.0 * den[...] * den[...] * stiffness / LOADS
    mom[3] = sum_arx2()
    sum_ary2 = sum_start(ary2, y_slot, y_peers, 3)
    get_b2.wait()
    get_part.wait()
    get_shp.wait()
    sens = part[f, 0:1, :] + got[0:1, :]
    total = sum_ary2()
    columns(step_sizes(total))

    def body(n, energies):
        rows = pl.ds(pl.multiple_of(n * ROWS, ROWS), ROWS)
        a, b = col[rows, 0:1], col[rows, 1:2]
        x = a * s0[rows, :] + b * bs[rows, :]
        out_h[0, 0, 0, rows, :] = x
        there = a * sp[rows, :] + b * bsp[rows, :].astype(F32)
        return (
            energies[0] + jnp.sum(x * x, axis=0, keepdims=True),
            energies[1] + jnp.sum(there * there, axis=0, keepdims=True),
        )

    zero = jnp.zeros((1, h0.shape[1]), F32)
    energies = lax.fori_loop(0, LOADS // ROWS, body, (zero, zero))
    for energy, table in zip(energies, (sh[f], shp[...])):
        wide = jnp.broadcast_to(energy.astype(BF16), (16, energy.shape[1]))
        sens = sens + times(wide, table)[0:1, :]
    out_g[0] = factor * sens
    close()


def place(a, b, c, x, y, z, sem):
    copies = [
        pltpu.make_async_copy(src, dst, sem.at[k])
        for k, (src, dst) in enumerate(((a, x), (b, y), (c, z)))
    ]
    for copy in copies:
        copy.start()
    for copy in copies:
        copy.wait()


def solution(mesh):
    nx, ny = mesh.shape["gx"], mesh.shape["gy"]
    zs = 8 if nx % 8 == 0 else 1
    xs = nx // zs

    def vm(*shape, dtype=F32):
        return pltpu.VMEM(shape, dtype)

    def bm(*shape):
        return pltpu.VMEM(shape, BF16)

    in_hbm = pl.BlockSpec(memory_space=pltpu.HBM)
    in_vmem = pl.BlockSpec(memory_space=pltpu.VMEM)
    sems = pltpu.SemaphoreType.DMA
    outs = (
        jax.ShapeDtypeStruct((1, 1, 1, 128, 768), F32),
        jax.ShapeDtypeStruct((1, 1, 1, 128, 256), F32),
        jax.ShapeDtypeStruct((1, 1, 128), F32),
    )

    def on_device(*args):
        results = pl.pallas_call(
            functools.partial(kernel, nx, ny, xs, zs),
            out_shape=outs,
            in_specs=[in_hbm] * 18,
            out_specs=(in_vmem,) * 3,
            scratch_shapes=[
                vm(128, 768), vm(128, 256), bm(768, 768), bm(256, 256),
                vm(4, 1, 768), vm(4, 1, 256), vm(2, 1, 768), vm(2, 1, 256),
                bm(768, 256), bm(768, 256), bm(2, 256, 128), bm(256, 128),
                vm(1, 128), vm(1, 128, dtype=jnp.int32), pltpu.SMEM((8,), F32),
                bm(128, 768), bm(5, 128, 768), vm(128, 768), bm(128, 768), bm(5, 64, 768),
                bm(128, 256), bm(5, 128, 256), vm(128, 256),
                vm(128, 512), bm(2, 128, 256), bm(10, 128, 256), vm(128, 512),
                vm(128, 256), vm(128, 256), vm(128, 256), bm(128, 256), bm(4, 64, 256),
                bm(128, 256),
                vm(128, 128), vm(128, 128), vm(5, 128, 128), vm(4, 8, 128),
                vm(nx, 8, 128), vm(ny * 2, 8, 128), vm(nx, 8, 128), vm(ny * 2, 8, 128),
                vm(128, 768), vm(128, 256), vm(2, 8, 128), vm(8, 128),
                sems((64,)), sems((4,)), sems((4,)), sems((40,)), sems((40,)),
                sems((4,)), sems((4,)), sems((3,)), sems((3,)),
            ],
            compiler_params=pltpu.CompilerParams(
                collective_id=0, has_side_effects=True, vmem_limit_bytes=32 * 1024 * 1024
            ),
        )(*(pltpu.with_memory_space_constraint(a, pltpu.HBM) for a in args))
        return pl.pallas_call(
            place,
            out_shape=outs,
            in_specs=[in_vmem] * 3,
            out_specs=[in_hbm] * 3,
            scratch_shapes=[sems((3,))],
        )(*(pltpu.with_memory_space_constraint(a, pltpu.VMEM) for a in results))

    block = P("gx", "gy", "phys", None, None)
    line = P("gx", "gy", "phys", None)
    both = P("gx", "gy", None)
    part = P("gx", "gy", "phys")
    return jax.shard_map(
        on_device,
        mesh=mesh,
        in_specs=(
            block, block, block, block, line, line, line, line, both, line, line, both,
            block, block, block, part, part, P(),
        ),
        out_specs=(block, block, part),
        check_vma=False,
    )
```

```python
import functools

import jax
import jax.numpy as jnp
from jax import lax
from jax.experimental import pallas as pl
from jax.experimental.pallas import tpu as pltpu
from jax.sharding import PartitionSpec as P

MESH = pl.DeviceIdType.MESH
F32 = jnp.float32
BF16 = jnp.bfloat16
ROWS = 16
LOADS = 128
HALF = LOADS // 2
PIECES = 4
PIECE = LOADS // PIECES
END = PIECE // 2


def ring(k, n):
    return min(k, n - k)


def remote(src, dst, send, recv, peer):
    return pltpu.make_async_remote_copy(
        src_ref=src, dst_ref=dst, send_sem=send, recv_sem=recv, device_id=peer, device_id_type=MESH
    )


class Once:
    def __init__(self, wait, group):
        self.pending = wait
        group.append(self)

    def wait(self):
        if self.pending is not None:
            self.pending()
            self.pending = None


def row_loop(body, count=LOADS, first=0):
    def step(n, carry):
        body(pl.ds(pl.multiple_of(first + n * ROWS, ROWS), ROWS))
        return carry

    lax.fori_loop(0, count // ROWS, step, 0)


def fold(x):
    return sum(x[:, k : k + 128] for k in range(0, x.shape[1], 128))


def lane_sums(parts):
    return lax.dot_general(
        jnp.ones((8, 128), F32), parts, (((1,), (1,)), ((), ())),
        precision=lax.Precision.HIGHEST, preferred_element_type=F32,
    )


def times(a, b):
    return jnp.dot(a, b, preferred_element_type=F32)


def times_t(a, b):
    return lax.dot_general(a, b, (((1,), (1,)), ((), ())), preferred_element_type=F32)


def step_sizes(total):
    rr, rw, ww, gw, hw = (total[k : k + 1, :] for k in range(5))
    alpha = rr / rw
    beta = (rr - 2.0 * alpha * rw + alpha * alpha * ww) / rr
    grow = 1.0 + beta
    curve = grow * grow * rw - 2.0 * grow * alpha * gw + alpha * alpha * hw
    second = beta * rr / curve
    return alpha + second * grow, -second * alpha


def kernel(
    nx, ny, xs, zs,
    ml, hl, mf, hf, md, hd, mx, my, mp, hx, hy, hp, cp, ms, hs, dn, ids, sc,
    out_m, out_h, out_g,
    r0, h0, zf, bf, mw, hw, mup, hup, cf, sm, sh, shp, den, mat, scale,
    q0, qn, w0, wb, wn, hb, hn, bh, uv, uvb, uvn, buv, s0, sp, bs, bsb, bsn, bsp,
    msc, col, pm, mom, arx1, ary1, arx2, ary2, xm, xh, part, got,
    lsem, wsend, wrecv, esend, erecv, asend, arecv, fsend, frecv,
):
    i, j, f = lax.axis_index("gx"), lax.axis_index("gy"), lax.axis_index("phys")
    low_x, high_x, low_y, high_y = i > 0, i < nx - 1, j > 0, j < ny - 1
    up_x = (jnp.minimum(i + 1, nx - 1), j, f)
    down_x = (jnp.maximum(i - 1, 0), j, f)
    up_y = (i, jnp.minimum(j + 1, ny - 1), f)
    down_y = (i, jnp.maximum(j - 1, 0), f)
    other = (i, j, 1 - f)
    target = (up_x, down_x, up_y, down_y, other)
    sends = (high_x, low_x, high_y, low_y, None)
    gets = (low_x, high_x, low_y, high_y, None)

    def guarded(cond, fn):
        if cond is None:
            fn()
        else:
            pl.when(cond)(fn)

    xi, zi = lax.div(i, zs), lax.rem(i, zs)
    offsets = [(a, b) for a in range(xs) for b in range(zs) if (a, b) != (0, 0)]
    offsets.sort(key=lambda o: -(ring(o[0], xs) + ring(o[1], zs)))
    x_peers = [(lax.rem(xi + a, xs) * zs + lax.rem(zi + b, zs), j, f) for a, b in offsets]
    yi, ci = f * (ny // 2) + lax.div(j, 2), lax.rem(j, 2)
    offsets = [(a, b) for a in range(ny) for b in range(2) if (a, b) != (0, 0)]
    offsets.sort(key=lambda o: -(ring(o[0], ny) + 0.1 * o[1]))
    y_peers = []
    for a, b in offsets:
        y = lax.rem(yi + a, ny)
        y_peers.append((i, lax.rem(y, ny // 2) * 2 + lax.rem(ci + b, 2), lax.div(y, ny // 2)))
    x_slot, y_slot = i, yi * 2 + ci

    finish = []

    def load(src, dst):
        copy = pltpu.make_async_copy(src, dst, lsem.at[len(finish)])
        copy.start()
        return Once(copy.wait, finish)

    def close():
        for piece in finish:
            piece.wait()

    pieces = [pl.ds(PIECE * c, PIECE) for c in range(PIECES)]
    get_r0 = [load(ml.at[0, 0, 0, piece], r0.at[piece]) for piece in pieces]
    barrier = pltpu.get_barrier_semaphore()
    for peer in y_peers + x_peers:
        pl.semaphore_signal(barrier, inc=1, device_id=peer, device_id_type=MESH)

    def exchange(stage, src_of, dst_of):
        receipts, departures = {}, {}

        def copy(d):
            k = stage * 5 + d
            return remote(src_of(d), dst_of(d), esend.at[k], erecv.at[k], target[d])

        def start(order=(4, 0, 1, 2, 3)):
            for d in order:
                guarded(sends[d], lambda: copy(d).start())
                receipts[d] = Once(lambda d=d: guarded(gets[d], copy(d).wait_recv), finish)
                departures[d] = Once(lambda d=d: guarded(sends[d], copy(d).wait_send), finish)

        def arrive(order=(0, 1, 2, 3)):
            for d in order:
                receipts[d].wait()

        def sent(order):
            for d in order:
                departures[d].wait()

        return start, arrive, sent

    low, high = pl.ds(0, HALF), pl.ds(HALF, HALF)
    mine = pl.ds(pl.multiple_of(f * HALF, HALF), HALF)
    yours = pl.ds(pl.multiple_of((1 - f) * HALF, HALF), HALF)
    half = (low, high, low, high, yours)
    q_sends = [
        exchange(s, lambda d, c=c: q0.at[pieces[c]], lambda d, c=c: qn.at[d, pieces[c]])
        for c, s in enumerate((0, 6, 8, 9)[:PIECES])
    ]

    def ends_of(d, c):
        shift = (0, END, 0, END, (1 - f) * END)[d]
        return pl.ds(pl.multiple_of(PIECE * c + shift, END), END)

    w_sends = [
        exchange(
            s,
            lambda d, c=c: wb.at[ends_of(d, c)],
            lambda d, c=c: wn.at[d, pl.ds(END * c, END)],
        )
        for c, s in enumerate((2, 7, 10, 11)[:PIECES])
    ]
    h_start, h_arrive, h_sent = exchange(1, lambda d: hb, lambda d: hn.at[d])
    u_start, u_arrive, u_sent = exchange(3, lambda d: uvb.at[0], lambda d: uvn.at[d])
    v_start, v_arrive, v_sent = exchange(5, lambda d: uvb.at[1], lambda d: uvn.at[5 + d])
    b_start, b_arrive, b_sent = exchange(
        4, lambda d: bsb.at[half[d]], lambda d: bsp.at[yours] if d == 4 else bsn.at[d]
    )

    def face_send(k, src, dst):
        copy = remote(src, dst, fsend.at[k], frecv.at[k], other)
        copy.start()
        Once(copy.wait_send, finish)
        return Once(copy.wait_recv, finish)

    for c, (start, _, _) in enumerate(q_sends):
        get_r0[c].wait()
        q0[pieces[c], :] = r0[pieces[c], :].astype(BF16)
        if c == 0:
            pl.semaphore_wait(barrier, len(x_peers) + len(y_peers))
        start()
    for d, there in enumerate(gets[:4]):
        @pl.when(jnp.logical_not(there))
        def _():
            for ref in (qn, wn, hn, uvn, bsn):
                ref[d] = jnp.zeros_like(ref[d])
            uvn[5 + d] = jnp.zeros_like(uvn[d])
    for d, there in ((0, high_x), (1, high_y)):
        @pl.when(jnp.logical_not(there))
        def _():
            mup[d] = jnp.zeros_like(mup[d])
            hup[d] = jnp.zeros_like(hup[d])

    small = [
        load(md.at[0, 0], mw.at[0]), load(mx.at[0, 0], mw.at[1]), load(my.at[0, 0], mw.at[2]),
        load(mp.at[0], mw.at[3]),
        load(hd.at[0, 0], hw.at[0]), load(hx.at[0, 0], hw.at[1]), load(hy.at[0, 0], hw.at[2]),
        load(hp.at[0], hw.at[3]),
    ]
    get_z = load(mf.at[0, 0, 0], zf)
    get_c = load(cp.at[0, 0, 0], cf)
    get_h = load(hl.at[0, 0, 0], h0)
    get_b = load(hf.at[0, 0, 0], bf)
    get_sm = load(ms.at[0, 0, 0], sm)
    get_sh = [load(hs.at[0, 0, 0, :, pl.ds(128 * k, 128)], sh.at[k]) for k in range(2)]
    get_last = [load(dn.at[0], den), load(ids.at[0], mat), load(sc, scale)]
    for copy in small:
        copy.wait()

    def weights(k):
        src, dst, peer = (
            (mw.at[1], mup.at[0], down_x), (mw.at[2], mup.at[1], down_y),
            (hw.at[1], hup.at[0], down_x), (hw.at[2], hup.at[1], down_y),
        )[k]
        return remote(src, dst, wsend.at[k], wrecv.at[k], peer)

    above = []
    for k in range(4):
        guarded((low_x, low_y)[k % 2], lambda: weights(k).start())
        Once(lambda k=k: guarded((low_x, low_y)[k % 2], lambda: weights(k).wait_send()), finish)
        above.append(
            Once(lambda k=k: guarded((high_x, high_y)[k % 2], lambda: weights(k).wait_recv()), finish)
        )
    mom[...] = jnp.zeros_like(mom)
    msc[...] = jnp.zeros_like(msc)

    get_z.wait()
    inner = times(q0[...], zf[...]).astype(BF16)
    w0[...] = times_t(inner, zf[...])
    get_c.wait()
    uv[:, :256] = times(q0[...], cf[...])
    uvb[0] = uv[:, :256].astype(BF16)
    get_h.wait()
    hb[...] = h0[...].astype(BF16)
    get_b.wait()
    bh[...] = times_t(times(hb[...], bf[...]).astype(BF16), bf[...])
    for copy in above:
        copy.wait()

    def near(total, w, up, values, nb, rows, cols=slice(None)):
        diag, wx, wy, wp = w[0], w[1], w[2], w[3]
        ux, uy = up[0], up[1]
        total = total + (diag + wx + ux + wy + uy + wp) * values
        total = total - wx * nb[0, rows, cols].astype(F32) - ux * nb[1, rows, cols].astype(F32)
        return total - wy * nb[2, rows, cols].astype(F32) - uy * nb[3, rows, cols].astype(F32)

    for c in range(PIECES):
        start, arrive, sent = q_sends[c]
        arrive()

        def body(rows):
            w0[rows, :] = near(w0[rows, :], mw, mup, q0[rows, :].astype(F32), qn, rows)

        row_loop(body, PIECE, PIECE * c)
        arrive((4,))

        def body(rows):
            w = w0[rows, :] - mw[3] * qn[4, rows, :].astype(F32)
            w0[rows, :] = w
            wb[rows, :] = w.astype(BF16)

        row_loop(body, PIECE, PIECE * c)
        if c == 0:
            q_sends[-1][2]((4,))
        w_sends[c][0]()
    u_start((0, 1))
    h_start((0, 1))
    uv[:, 256:] = times(wb[...], cf[...])
    uvb[1] = uv[:, 256:].astype(BF16)
    v_start((0, 1))

    def moments(k, r, w, b, inner, weight):
        def body(rows):
            rv, wv, bv = r[rows, :], w[rows, :], b[rows, :].astype(F32)
            iv = inner[rows, :]
            pm[0, rows, :] = fold(rv * rv)
            pm[1, rows, :] = fold(rv * wv)
            pm[2, rows, :] = fold(wv * wv)
            pm[3, rows, :] = fold(bv * wv)
            pm[4, rows, :] = fold(weight[0] * bv * bv + iv * iv)

        row_loop(body)
        sums = lane_sums(pm[:4].reshape(4 * LOADS, 128))
        for n in range(4):
            mom[k, n : n + 1, :] = sums[0:1, n * LOADS : (n + 1) * LOADS]

    def moments_end(k):
        mom[k, 4:5, :] = lane_sums(pm[4])[0:1, :]

    def edges(b, nb, weight, up, first, there, count):
        ends = jnp.where(low_x, 0.0, weight[1]) + jnp.where(low_y, 0.0, weight[2])

        def body(n, carry):
            rows = pl.ds(pl.multiple_of(there + n * ROWS, ROWS), ROWS)
            lower = pl.ds(pl.multiple_of(first + n * ROWS, ROWS), ROWS)
            bv = b[lower, :].astype(F32)
            dx, dy = bv - nb[0, rows, :].astype(F32), bv - nb[2, rows, :].astype(F32)
            pm[4, lower, :] += fold(weight[1] * dx * dx + weight[2] * dy * dy)
            upper = pl.ds(pl.multiple_of(first + count + n * ROWS, ROWS), ROWS)
            bv = b[upper, :].astype(F32)
            dx, dy = bv - nb[1, rows, :].astype(F32), bv - nb[3, rows, :].astype(F32)
            pm[4, upper, :] += fold(up[0] * dx * dx + up[1] * dy * dy + ends * bv * bv)
            return carry

        lax.fori_loop(0, count // ROWS, body, 0)

    def face_edges(b, other_face, weight, first, there, count):
        def body(n, carry):
            rows = pl.ds(pl.multiple_of(there + n * ROWS, ROWS), ROWS)
            own = pl.ds(pl.multiple_of(first + f * count + n * ROWS, ROWS), ROWS)
            d = b[own, :].astype(F32) - other_face(rows, own).astype(F32)
            pm[4, own, :] += fold(weight[3] * d * d)
            return carry

        lax.fori_loop(0, count // ROWS, body, 0)

    def sum_start(buf, slot, peers, k):
        for peer in peers:
            remote(mom.at[k], buf.at[slot], asend.at[k], arecv.at[k], peer).start()
        buf[slot] = mom[k]
        rest = buf.at[pl.ds(0, buf.shape[0] - 1)]
        arrived = Once(lambda: pltpu.make_async_copy(rest, rest, arecv.at[k]).wait(), finish)
        Once(lambda: pltpu.make_async_copy(rest, rest, asend.at[k]).wait(), finish)

        def end():
            arrived.wait()
            return jnp.sum(buf[...], axis=0)

        return end

    xm[...] = times(wb[...], zf[...])
    moments(0, r0, w0, wb, xm, mw)
    w_sends[-1][2]((4,))
    u_start((4, 2, 3))
    v_start((4, 2, 3))
    for c in range(PIECES):
        w_sends[c][1]()
        edges(wb, wn, mw, mup, PIECE * c, END * c, END)
        w_sends[c][1]((4,))
        face_edges(wb, lambda rows, own: wn[4, rows, :], mw, PIECE * c, END * c, END)
    moments_end(0)
    sum_arx1 = sum_start(arx1, x_slot, x_peers, 0)
    h_start((4, 2, 3))

    for k in range(2):
        cols = slice(256 * k, 256 * k + 256)
        buv[:, cols] = times_t(times(uvb[k], bf[...]).astype(BF16), bf[...])
    mom[1] = sum_arx1()
    sum_ary1 = sum_start(ary1, y_slot, y_peers, 1)
    h_arrive((0, 1, 2, 3, 4))

    def body(rows):
        total = near(bh[rows, :], hw, hup, hb[rows, :].astype(F32), hn, rows)
        bh[rows, :] = total - hw[3] * hn[4, rows, :].astype(F32)

    row_loop(body)
    u_arrive((0, 1, 2, 3, 4))
    v_arrive((0, 1, 2, 3, 4))

    def body(rows):
        for k in range(2):
            cols = slice(256 * k, 256 * k + 256)
            there = uvn.at[5 * k : 5 * k + 5]
            total = near(buv[rows, cols], hw, hup, uvb[k, rows, :].astype(F32), there, rows)
            buv[rows, cols] = total - hw[3] * there[4, rows, :].astype(F32)

    row_loop(body)

    def columns(pair):
        msc[0:1, :] = pair[0]
        msc[1:2, :] = pair[1]
        col[...] = jnp.transpose(msc[...])

    total = sum_ary1()
    columns(step_sizes(total))

    def body(rows):
        a, b = col[rows, 0:1], col[rows, 1:2]
        image = bh[rows, :] - a * buv[rows, :256] - b * buv[rows, 256:]
        bs[rows, :] = image
        bsb[rows, :] = image.astype(BF16)

    row_loop(body)
    b_start()

    def body(n, energy):
        rows = pl.ds(pl.multiple_of(n * ROWS, ROWS), ROWS)
        a, b = col[rows, 0:1], col[rows, 1:2]
        s0[rows, :] = h0[rows, :] - a * uv[rows, :256] - b * uv[rows, 256:]
        sp[rows, :] = (
            hn[4, rows, :].astype(F32)
            - a * uvn[4, rows, :].astype(F32)
            - b * uvn[9, rows, :].astype(F32)
        )
        x = a * r0[rows, :] + b * w0[rows, :]
        out_m[0, 0, 0, rows, :] = x
        return energy + jnp.sum(x * x, axis=0, keepdims=True)

    energy = lax.fori_loop(0, LOADS // ROWS, body, jnp.zeros((1, r0.shape[1]), F32))
    get_sm.wait()
    sens = times(jnp.broadcast_to(energy.astype(BF16), (16, energy.shape[1])), sm[...])
    part[0] = sens[:8, :128]
    part[1] = sens[:8, 128:]
    xh[...] = times(bsb[...], bf[...])
    moments(2, s0, bs, bsb, xh, hw)
    b_arrive()
    edges(bsb, bsn, hw, hup, 0, 0, HALF)
    b_arrive((4,))
    face_edges(bsb, lambda rows, own: bsp[own, :], hw, 0, 0, HALF)
    moments_end(2)
    sum_arx2 = sum_start(arx2, x_slot, x_peers, 2)
    get_b2 = face_send(0, bsb.at[mine], bsp.at[mine])
    get_part = face_send(2, part.at[1 - f], got)
    for copy in get_sh:
        copy.wait()
    get_shp = face_send(1, sh.at[1 - f], shp)
    for copy in get_last:
        copy.wait()
    kinds = mat[...]
    stiffness = jnp.zeros(kinds.shape, F32)
    for k in range(scale.shape[0]):
        stiffness = jnp.where(kinds == k, scale[k], stiffness)
    factor = -3.0 * den[...] * den[...] * stiffness / LOADS
    mom[3] = sum_arx2()
    sum_ary2 = sum_start(ary2, y_slot, y_peers, 3)
    get_b2.wait()
    get_part.wait()
    get_shp.wait()
    sens = part[f, 0:1, :] + got[0:1, :]
    total = sum_ary2()
    columns(step_sizes(total))

    def body(n, energies):
        rows = pl.ds(pl.multiple_of(n * ROWS, ROWS), ROWS)
        a, b = col[rows, 0:1], col[rows, 1:2]
        x = a * s0[rows, :] + b * bs[rows, :]
        out_h[0, 0, 0, rows, :] = x
        there = a * sp[rows, :] + b * bsp[rows, :].astype(F32)
        return (
            energies[0] + jnp.sum(x * x, axis=0, keepdims=True),
            energies[1] + jnp.sum(there * there, axis=0, keepdims=True),
        )

    zero = jnp.zeros((1, h0.shape[1]), F32)
    energies = lax.fori_loop(0, LOADS // ROWS, body, (zero, zero))
    for energy, table in zip(energies, (sh[f], shp[...])):
        wide = jnp.broadcast_to(energy.astype(BF16), (16, energy.shape[1]))
        sens = sens + times(wide, table)[0:1, :]
    out_g[0] = factor * sens
    close()


def place(a, b, c, x, y, z, sem):
    copies = [
        pltpu.make_async_copy(src, dst, sem.at[k])
        for k, (src, dst) in enumerate(((a, x), (b, y), (c, z)))
    ]
    for copy in copies:
        copy.start()
    for copy in copies:
        copy.wait()


def solution(mesh):
    nx, ny = mesh.shape["gx"], mesh.shape["gy"]
    zs = 8 if nx % 8 == 0 else 1
    xs = nx // zs

    def vm(*shape, dtype=F32):
        return pltpu.VMEM(shape, dtype)

    def bm(*shape):
        return pltpu.VMEM(shape, BF16)

    in_hbm = pl.BlockSpec(memory_space=pltpu.HBM)
    in_vmem = pl.BlockSpec(memory_space=pltpu.VMEM)
    sems = pltpu.SemaphoreType.DMA
    outs = (
        jax.ShapeDtypeStruct((1, 1, 1, 128, 768), F32),
        jax.ShapeDtypeStruct((1, 1, 1, 128, 256), F32),
        jax.ShapeDtypeStruct((1, 1, 128), F32),
    )

    def on_device(*args):
        results = pl.pallas_call(
            functools.partial(kernel, nx, ny, xs, zs),
            out_shape=outs,
            in_specs=[in_hbm] * 18,
            out_specs=(in_vmem,) * 3,
            scratch_shapes=[
                vm(128, 768), vm(128, 256), bm(768, 768), bm(256, 256),
                vm(4, 1, 768), vm(4, 1, 256), vm(2, 1, 768), vm(2, 1, 256),
                bm(768, 256), bm(768, 256), bm(2, 256, 128), bm(256, 128),
                vm(1, 128), vm(1, 128, dtype=jnp.int32), pltpu.SMEM((8,), F32),
                bm(128, 768), bm(5, 128, 768), vm(128, 768), bm(128, 768), bm(5, 64, 768),
                bm(128, 256), bm(5, 128, 256), vm(128, 256),
                vm(128, 512), bm(2, 128, 256), bm(10, 128, 256), vm(128, 512),
                vm(128, 256), vm(128, 256), vm(128, 256), bm(128, 256), bm(4, 64, 256),
                bm(128, 256),
                vm(128, 128), vm(128, 128), vm(5, 128, 128), vm(4, 8, 128),
                vm(nx, 8, 128), vm(ny * 2, 8, 128), vm(nx, 8, 128), vm(ny * 2, 8, 128),
                vm(128, 768), vm(128, 256), vm(2, 8, 128), vm(8, 128),
                sems((128,)), sems((4,)), sems((4,)), sems((60,)), sems((60,)),
                sems((4,)), sems((4,)), sems((3,)), sems((3,)),
            ],
            compiler_params=pltpu.CompilerParams(
                collective_id=0, has_side_effects=True, vmem_limit_bytes=32 * 1024 * 1024
            ),
        )(*(pltpu.with_memory_space_constraint(a, pltpu.HBM) for a in args))
        return pl.pallas_call(
            place,
            out_shape=outs,
            in_specs=[in_vmem] * 3,
            out_specs=[in_hbm] * 3,
            scratch_shapes=[sems((3,))],
        )(*(pltpu.with_memory_space_constraint(a, pltpu.VMEM) for a in results))

    block = P("gx", "gy", "phys", None, None)
    line = P("gx", "gy", "phys", None)
    both = P("gx", "gy", None)
    part = P("gx", "gy", "phys")
    return jax.shard_map(
        on_device,
        mesh=mesh,
        in_specs=(
            block, block, block, block, line, line, line, line, both, line, line, both,
            block, block, block, part, part, P(),
        ),
        out_specs=(block, block, part),
        check_vma=False,
    )
```
